128 devices in a mesh: gx: 16 (over z, x), gy: 8 (over y, core).
Axes of the slice: x: 4, y: 4, z: 4, core: 2. Of those that a mesh axis runs over, the one named last changes fastest.
Arguments:
- normals: float32 [16384, 2, 256], P(('gx', 'gy')), may hold values from -24 to 24
- fractions: float32 [16384, 2, 256], P(('gx', 'gy')), may hold values from 0.01 to 0.99
- offsets: int32 [16384, 256], P(('gx', 'gy')), may hold values from 0 to 8062, as said below
- owner: int32 [16384, 1], P(('gx', 'gy')), may hold values from 0 to 127; in each aligned block of 128 rows (0 to 127, 128 to 255, ...) at most 2 rows name the same one
- brick: int32 [16384], P(('gx', 'gy')), may hold values from 0 to 31
- fill: int32 [16384], P(('gx', 'gy')), may hold values from 1 to 256, 2621440 in all
Outputs:
- indicator: float32 [8, 2048, 2048], P('gy', None, 'gx')
- gradient: float32 [2, 8, 2048, 2048], P(None, 'gy', None, 'gx')
The draws below stay inside these ranges and needn't reach their ends.
Inputs may be any that keep to these rules, and one draw needn't show every extreme that they name: Among the blocks held by one device no owner is named by more than 2 blocks. `offsets`: each offset is (iz * 8 + iy) * 128 + ix with iz below 8, iy at most 6 and ix at most 126; of the 256 points of one block, live or padding, no plane holds more than 64, and every block has one plane with exactly 64. Points of a block at positions from its fill on are padding.
All inputs are finite; a program needn't handle non-finite values.
Results may differ from the reference program's by a relative error of at most 0.0023.
Values sent between devices are 32-bit elements; how exact they have to be, the bound alone decides.
No kernel may reach another device: no remote copies, remote signals or barrier semaphores. Data moves between devices by JAX's collectives and lax.ppermute only.
A program may use at most 64 MiB of HBM per device.

```python
import math
import jax
import jax.numpy as jnp
import numpy as np
from jax import lax

NX = 2048
NY = 2048
Z = 8
P_SIZE = 256
BX = 128
BY = 8
BLK_DEV = 128
CX = 128
CY = 256
CAP = 2
BLOCKS = 16384
BRICKS_DEV = 32
N_GY = 8
DEVICES = 128


def draw_offsets(key, part):
    key_perm, key_spread, key_shift, key_row, key_col = jax.random.split(key, 5)
    spread = P_SIZE // Z
    scores = jax.random.randint(key_perm, (BLOCKS, P_SIZE), 0, 1048576, dtype=jnp.int32) * P_SIZE + jnp.arange(P_SIZE, dtype=jnp.int32)[None, :]
    order_rank = jnp.argsort(scores, axis=1, stable=True).astype(jnp.int32)
    jitter = jax.random.randint(key_spread, (BLOCKS, Z), 0, spread + 1, dtype=jnp.int32)
    jitter = jitter.at[:, 0].set(spread).at[:, 1].set(0)
    lengths = spread + jitter - jnp.roll(jitter, -1, axis=1)
    bounds = jnp.cumsum(lengths, axis=1).astype(jnp.int32)
    segment = jnp.zeros((BLOCKS, P_SIZE), jnp.int32)
    for index in range(Z - 1):
        segment = segment + (order_rank >= bounds[:, index:index + 1]).astype(jnp.int32)
    shift_by = jax.random.randint(key_shift, (BLOCKS, 1), 0, Z, dtype=jnp.int32)
    plane_ids = (segment + shift_by) % Z
    row_ids = jax.random.randint(key_row, (BLOCKS, P_SIZE), 0, BY - 1, dtype=jnp.int32)
    col_ids = jax.random.randint(key_col, (BLOCKS, P_SIZE), 0, BX - 1, dtype=jnp.int32)
    return (plane_ids * BY + row_ids) * BX + col_ids


def touch_ends(entries, rng, least, largest):
    spot = [jax.random.randint(jax.random.fold_in(rng, axis), (), 0, length) for axis, length in enumerate(entries.shape)]
    main_axis = entries.shape.index(max(entries.shape))
    next_to = spot[:main_axis] + [(spot[main_axis] + 1) % entries.shape[main_axis]] + spot[main_axis + 1:]
    return entries.at[tuple(spot)].set(least).at[tuple(next_to)].set(largest)


def block_scale(rng, extent, cuts, low, top_value):
    gain, own = 1.0, jax.random.fold_in(rng, 6)
    for position, parts in cuts:
        heights = jnp.exp(jax.random.uniform(jax.random.fold_in(own, position), (parts,), jnp.float32, low / len(cuts), top_value / len(cuts)))
        gain = gain * jnp.repeat(heights, extent[position] // parts).reshape([-1 if axis == position else 1 for axis in range(len(extent))])
    return gain


def length_profile(count, total, bound, skew):
    portions = [(1 << 20) // math.isqrt(standing ** skew) + 1 for standing in range(2, count + 1)]
    spare, given = total - bound - (count - 1), [1] * (count - 1)
    while spare > 0:
        candidates = [i for i in range(count - 1) if given[i] < bound]
        whole, left = sum([portions[i] for i in candidates]), spare
        for i in candidates:
            more = min(bound - given[i], max(1, left * portions[i] // whole), spare)
            given[i] = given[i] + more
            spare = spare - more
    return np.array([bound] + given)


def uneven(own_key, count, total, limit, skew):
    if count == 2:
        one = jax.random.randint(own_key, (), max(1, total - limit), min(limit, total - 1) + 1)
        return jnp.stack([one, total - one])
    sizes = jnp.asarray(length_profile(count, total, limit, skew), jnp.int32)
    pairs = (count - 1) // 2
    giver, sink = sizes[1:1 + 2 * pairs:2], sizes[2:2 + 2 * pairs:2]
    margin = jnp.minimum(giver - 1, limit - sink)
    passed = jax.random.randint(jax.random.fold_in(own_key, 1), (pairs,), 0, 1 << 20) % (margin + 1)
    sizes = sizes.at[1:1 + 2 * pairs:2].set(giver - passed).at[2:2 + 2 * pairs:2].set(sink + passed)
    return sizes[jax.random.permutation(jax.random.fold_in(own_key, 2), count)]


def assign_block(own_key, own, number, rows, amount, top, most, skew):
    sequence = jax.random.permutation(own_key, amount)
    packed, usual = shares(amount, rows * top, most, skew, True), shares(amount, rows * top, most, skew, False)
    places = jnp.arange(amount)

    def named(sizes, rotation):
        used = int((sizes > 0).sum())
        fixed = max(1, used // 4)
        passed = fixed + (places - fixed + rotation * (used - fixed)) % max(1, amount - fixed)
        return jnp.zeros((amount,), jnp.int32).at[sequence[jnp.where(places < fixed, places, passed)]].set(jnp.asarray(sizes, jnp.int32))

    sizes = jnp.where(number % 4 == 0, named(packed, number // 4), named(usual, number - number // 4 - 1))
    mixed = jax.random.permutation(jax.random.fold_in(own, 3), amount)
    source_of, sink = mixed[0:amount // 2 * 2:2], mixed[1:amount // 2 * 2:2]
    slack = jnp.minimum(sizes[source_of] - 1, most - sizes[sink]) // 2
    slack = jnp.where((source_of == sequence[0]) | (sink == sequence[0]) | (sizes[sink] == 0), 0, jnp.maximum(slack, 0))
    passed = jax.random.randint(jax.random.fold_in(own, 4), (amount // 2,), 0, 1 << 20) % (slack + 1)
    sizes = sizes.at[source_of].add(-passed).at[sink].add(passed)
    labels = jnp.searchsorted(jnp.cumsum(sizes), jnp.arange(rows * top), side="right").astype(jnp.int32)
    table = labels.reshape(top, rows).T
    table = table[jax.random.permutation(jax.random.fold_in(own, 1), rows)]
    rotation = jax.random.randint(jax.random.fold_in(own, 2), (rows, 1), 0, top)
    return jnp.take_along_axis(table, (jnp.arange(top)[None, :] + rotation) % top, axis=1)


def shares(count, total, reach, lean, full):
    portions = [(1 << 20) // math.isqrt(standing ** lean) + 1 for standing in range(1, count + 1)]
    largest = reach if full else min(reach, max(-(-total // count), total * portions[0] // sum(portions)))
    least = 1 if total - largest >= count - 1 else 0
    counts, surplus = [largest] + [least] * (count - 1), total - largest - least * (count - 1)
    while surplus > 0:
        candidates = [i for i in range(1, count) if counts[i] < largest] or [i for i in range(1, count) if counts[i] < reach]
        whole, remaining = sum([portions[i] for i in candidates]), surplus
        for i in candidates:
            extra = min(reach - counts[i], max(1, remaining * portions[i] // whole), surplus)
            counts[i] = counts[i] + extra
            surplus = surplus - extra
    return np.array(counts)


def bell_draw(rng, dims, scale, limit, shards=(), kind=jnp.bfloat16):
    result = scale * jax.random.normal(rng, dims, jnp.float32)
    if shards:
        result = result * block_scale(rng, dims, shards, -0.22, 0.18)
    return jnp.clip(result, -limit, limit).astype(kind)


def setup_inputs(seed: int = 0) -> dict:
    key_list = jax.random.split(jax.random.key(seed), 7)
    normals = bell_draw(key_list[0], (BLOCKS, 2, P_SIZE), 4.0, 24.0, ((0, 128),), jnp.float32)
    fractions = jnp.clip(0.01 + 0.98 * jax.random.uniform(key_list[1], (BLOCKS, 2, P_SIZE), jnp.float32) ** block_scale(key_list[1], (BLOCKS, 2, P_SIZE), ((0, 128),), -0.2, 0.2), 0.01, 0.99)
    offsets = draw_offsets(jax.random.fold_in(key_list[6], 71), 0)
    owner_keys = jax.random.split(jax.random.fold_in(key_list[3], 1), BLOCKS // BLK_DEV)
    owner_turns = jax.random.permutation(jax.random.fold_in(key_list[3], 3), BLOCKS // BLK_DEV)
    owner = jax.vmap(lambda own, number: assign_block(jax.random.fold_in(key_list[3], 2), own, number, BLK_DEV, DEVICES, 1, CAP, 2))(owner_keys, owner_turns).reshape((BLOCKS, 1))
    brick = touch_ends(jax.random.randint(key_list[4], (BLOCKS,), 0, BRICKS_DEV), jax.random.fold_in(key_list[4], 1), 0, BRICKS_DEV - 1).astype(jnp.int32)
    fill = uneven(key_list[5], BLOCKS, BLOCKS * P_SIZE * 5 // 8, P_SIZE, 1).astype(jnp.int32)
    return {"normals": normals, "fractions": fractions, "offsets": offsets, "owner": owner, "brick": brick, "fill": fill}


ALPHA = 4e-6


def reference(normals, fractions, offsets, owner, brick, fill):
    column_bricks = CX // BX
    live_mask = (jnp.arange(P_SIZE, dtype=jnp.int32)[None, :] < fill[:, None]).astype(jnp.float32)
    device_ids = owner[:, 0]
    x_base = (device_ids // N_GY) * CX + (brick % column_bricks) * BX
    y_base = (device_ids % N_GY) * CY + (brick // column_bricks) * BY
    plane_ids = offsets // (BY * BX)
    inside = offsets % (BY * BX)
    row_ids = y_base[:, None] + inside // BX
    col_ids = x_base[:, None] + inside % BX
    normal_x = normals[:, 0, :] * live_mask
    normal_y = normals[:, 1, :] * live_mask
    frac_x = fractions[:, 0, :]
    frac_y = fractions[:, 1, :]
    slopes = (1.0, -1.0)
    spline_x = (1.0 - frac_x, frac_x)
    spline_y = (1.0 - frac_y, frac_y)
    source = jnp.zeros((Z * NY * NX,), jnp.float32)
    for step_x in range(2):
        for step_y in range(2):
            weight = normal_x * slopes[step_x] * spline_y[step_y] + normal_y * spline_x[step_x] * slopes[step_y]
            flat_index = (plane_ids * NY + row_ids + step_y) * NX + col_ids + step_x
            source = source.at[flat_index.reshape(-1)].add(weight.reshape(-1))
    source = source.reshape(Z, NY, NX)
    freq_x = jnp.arange(NX, dtype=jnp.int32)
    freq_y = jnp.arange(NY, dtype=jnp.int32)
    fold_x = jnp.minimum(freq_x, NX - freq_x).astype(jnp.float32)
    fold_y = jnp.minimum(freq_y, NY - freq_y).astype(jnp.float32)
    part_x = -4.0 * jnp.square(jnp.sin(math.pi * fold_x / NX))
    part_y = -4.0 * jnp.square(jnp.sin(math.pi * fold_y / NY))
    operator_symbol = part_y[:, None] + part_x[None, :] - ALPHA
    nyquist = (freq_y[:, None] == NY // 2) | (freq_x[None, :] == NX // 2)
    response = jnp.where(nyquist, 0.0, 1.0 / operator_symbol)

    def solve_plane(plane):
        return jnp.real(jnp.fft.ifft2(jnp.fft.fft2(plane) * response)).astype(jnp.float32)

    indicator = lax.map(solve_plane, source)
    grad_x = jnp.roll(indicator, -1, axis=2) - indicator
    grad_y = jnp.roll(indicator, -1, axis=1) - indicator
    return indicator, jnp.stack([grad_x, grad_y])
```

```python
import functools
import math

import jax
import jax.numpy as jnp
import numpy as np
from jax import lax
from jax.experimental import pallas as pl
from jax.experimental.pallas import tpu as pltpu
from jax.sharding import PartitionSpec as P

NX = 2048
NY = 2048
Z = 8
BX = 128
BY = 8
P_SIZE = 256
GX = 16
GY = 8
DEV = GX * GY
ALPHA = 4e-06
SLOTS = 8
F32 = jnp.float32
BF16 = jnp.bfloat16
C1 = math.cos(math.pi / 8)
C2 = math.cos(math.pi / 4)
C3 = math.cos(3 * math.pi / 8)
INTERPRET = False


def np_split(values, parts):
    pieces = []
    rest = np.asarray(values, np.float64)
    for _ in range(parts):
        piece = rest.astype(BF16)
        pieces.append(piece)
        rest = rest - piece.astype(np.float64)
    return pieces


def slot_rows():
    ky = np.zeros((SLOTS, 256), np.int64)
    k2 = np.arange(128)
    half = np.arange(64)
    ky[0] = np.concatenate([16 * half, 16 * half, 8 + 16 * half, 8 + 16 * half])
    for slot in range(1, SLOTS):
        ky[slot] = np.concatenate([slot + 16 * k2, slot + 16 * k2])
    return ky


@functools.lru_cache(None)
def tables():
    ky = slot_rows()
    b = np.arange(128)
    fwd = np.zeros((SLOTS, 256, 256))
    weight = np.full((SLOTS, 256), 2.0 / NY)
    half = np.arange(64)
    for part in range(2):
        freq = part * 8 + 16 * half
        theta = 2 * np.pi * ((freq[:, None] * b[None, :]) % NY) / NY
        fwd[0, part * 128 : part * 128 + 64, part * 128 : part * 128 + 128] = np.cos(theta)
        fwd[0, part * 128 + 64 : part * 128 + 128, part * 128 : part * 128 + 128] = -np.sin(theta)
    weight[0, 0] = 1.0 / NY
    for slot in range(1, SLOTS):
        freq = slot + 16 * np.arange(128)
        theta = 2 * np.pi * ((freq[:, None] * b[None, :]) % NY) / NY
        cos, sin = np.cos(theta), np.sin(theta)
        fwd[slot] = np.block([[cos, sin], [-sin, cos]])
    inv = np.transpose(fwd, (0, 2, 1)) * weight[:, None, :]
    c = 4 * np.sin(np.pi * np.minimum(ky, NY - ky) / NY) ** 2 + ALPHA
    j = np.arange(1, 129)
    mu = 4 * np.sin(np.pi * j / 258) ** 2
    resp = -1.0 / (mu[None, None, :] + c[:, :, None])
    x = np.arange(128)
    sine = np.sqrt(2 / 129) * np.sin(np.pi * (x[:, None] + 1) * j[None, :] / 129)
    alt = ((-1.0) ** x) @ sine
    edge = np.zeros((8, 128))
    edge[0], edge[1], edge[2] = sine[0], sine[127], alt
    nyq = 1.0 / (-4.0 - c)
    root = np.sqrt(c * (c + 4))
    big = 1 + c / 2 + root / 2
    logr = -np.log(big)

    def green(n):
        n = n % NX
        return -(np.exp(logr * n) + np.exp(logr * (NX - n))) / (root * (1 - np.exp(logr * NX)))

    link0 = np.zeros((GX, SLOTS, 4, 256))
    link1 = np.zeros((GX, SLOTS, 4, 256))
    for n in range(GX):
        link0[n, :, 0] = -green(128 * n)
        link1[n, :, 0] = -green(128 * (n - 1) - 1) + (1.0 if n == 1 else 0.0)
        link0[n, :, 1] = -green(128 * (n + 1) + 1) + (1.0 if n == GX - 1 else 0.0)
        link1[n, :, 1] = -green(128 * n)
    fh, fm, fl = np_split(fwd, 3)
    ih, im = np_split(inv, 2)
    sh, sm, sl = np_split(sine, 3)
    ss = np.block([[sh, sm], [sh, sm]])
    s2 = np.concatenate([sl, sh], axis=0)
    eh, em, el = np_split(edge, 3)
    edges = np.concatenate([eh, eh, em, em, eh, el], axis=1)
    diff = np.concatenate([sine[:, 1:], np.zeros((128, 1))], axis=1) - sine
    back = np.concatenate([sine.T, np.concatenate([sine.T[:, 1:], np.zeros((128, 1))], axis=1) - sine.T], axis=1)
    bh, bm = np_split(back, 2)
    back1 = np.concatenate([bh, bh], axis=0)
    rank = np.zeros((4, 384))
    rank[0, 0:128] = sine[0]
    rank[1, 0:128] = sine[127]
    rank[2, 128:256] = alt
    rank[1, 256 + 127] = 1.0
    rank[2, 256 + 127] = -1.0
    rh, rm = np_split(rank, 2)
    ranks = np.concatenate([rh, rh, rm, np.zeros((4, 384), BF16)], axis=0)
    f = np.float32
    return dict(
        fh=fh, fm=fm, fl=fl, ih=ih, im=im, ss=ss, s2=s2, edges=edges, resp=resp.astype(f),
        nyq=nyq.reshape(SLOTS, 1, 256).astype(f), link0=link0.astype(f), link1=link1.astype(f),
        back1=back1, back2=bm, ranks=ranks,
    )


def split2(value):
    high = value.astype(BF16)
    return high, (value - high.astype(F32)).astype(BF16)


def split3(value):
    high = value.astype(BF16)
    rest = value - high.astype(F32)
    mid = rest.astype(BF16)
    return high, mid, (rest - mid.astype(F32)).astype(BF16)


def dot(left, right):
    return jnp.dot(left, right, preferred_element_type=F32)


def pack_kernel(owner, brick, fill, normals, fractions, offsets, send, counts):
    blocks = normals.shape[0]

    def clear(d, carry):
        counts[d] = 0
        send[d, 4] = jnp.full((4, 128), -1.0, F32)
        return carry

    lax.fori_loop(0, DEV, clear, 0, unroll=8)
    lane = lax.broadcasted_iota(jnp.int32, (2, 256), 1)
    row4 = lax.broadcasted_iota(jnp.int32, (4, 128), 0)

    def one(b, carry):
        d = owner[b]
        slot = counts[d]
        counts[d] = slot + 1
        live = jnp.where(lane < fill[b], normals[b], 0.0)
        frac = fractions[b]
        send[d, 2 * slot] = jnp.concatenate([live[:, :128], live[:, 128:]], axis=0)
        send[d, 2 * slot + 1] = jnp.concatenate(
            [frac[1:2, :128], frac[0:1, :128], frac[1:2, 128:], frac[0:1, 128:]], axis=0
        )
        cell = (offsets[pl.ds(b, 1), :] + brick[b] * (Z * BY * BX)).astype(F32)
        two = jnp.concatenate([cell[:, :128], cell[:, 128:]], axis=0)
        send[d, 4] = jnp.where(row4 // 2 == slot, jnp.concatenate([two, two], axis=0), send[d, 4])
        return carry

    lax.fori_loop(0, blocks, one, 0, unroll=4)


def splat_kernel(first, recv, out, acc):
    bricks = acc.shape[0]

    def clear(l, carry):
        acc[l] = jnp.zeros(acc.shape[1:], F32)
        return carry

    lax.fori_loop(0, bricks, clear, 0)
    rows = lax.broadcasted_iota(jnp.int32, (64, 128), 0)
    cols = lax.broadcasted_iota(jnp.int32, (128, 128), 0)

    def spread(row, matrix):
        return jnp.broadcast_to(row, matrix.shape)

    def one_slot(d, slot):
        cell2 = recv[d, 4][2 * slot : 2 * slot + 2].astype(jnp.int32)
        norm = recv[d, 2 * slot]
        frac = recv[d, 2 * slot + 1]
        filled = first[2 * d + slot] >= 0
        norm = jnp.where(filled, norm, 0.0)
        frac = jnp.where(filled, frac, 0.0)
        far = norm * frac
        near = norm * (1.0 - frac)
        near_h = near.astype(BF16).astype(F32)
        far_h = far.astype(BF16).astype(F32)
        near_l = near - near_h
        far_l = far - far_h
        line2 = (cell2 >> 7) & 63
        col2 = cell2 & 127
        high, low, right = [], [], []
        for half in range(2):
            line = spread(line2[half : half + 1], rows)
            here = line == rows
            below = line + 1 == rows
            x = 2 * half
            for parts, near_v, far_v in ((high, near_h, far_h), (low, near_l, far_l)):
                flux_x = jnp.where(
                    here,
                    spread(near_v[x : x + 1], rows),
                    jnp.where(below, spread(far_v[x : x + 1], rows), 0.0),
                )
                flux_y0 = jnp.where(here, spread(near_v[x + 1 : x + 2], rows), 0.0)
                flux_y1 = jnp.where(here, spread(far_v[x + 1 : x + 2], rows), 0.0)
                parts.append(
                    jnp.concatenate(
                        [flux_x.astype(BF16), flux_y0.astype(BF16), flux_y1.astype(BF16)], axis=0
                    )
                )
            right.append((spread(col2[half : half + 1], cols) == cols).astype(F32).astype(BF16))
        left = jnp.concatenate(high, axis=1)
        left_low = jnp.concatenate(low, axis=1)
        right = jnp.concatenate(right, axis=1)
        dims = (((1,), (1,)), ((), ()))
        piece = lax.dot_general(left, right, dims, preferred_element_type=F32)
        return piece + lax.dot_general(left_low, right, dims, preferred_element_type=F32)

    def one(d, carry):
        pieces = [one_slot(d, 0), one_slot(d, 1)]
        for slot in range(2):
            l = jnp.maximum(first[2 * d + slot], 0) >> 13
            acc[l] += pieces[slot]
        return carry

    lax.fori_loop(0, DEV, one, 0)

    def finish(l, carry):
        flux_x = acc[l, 0:64].reshape(Z, BY, 128)
        flux_y = (acc[l, 64:128] + pltpu.roll(acc[l, 128:192], 1, axis=1)).reshape(Z, BY, 128)
        moved_x = pltpu.roll(acc[l, 0:64], 1, axis=1).reshape(Z, BY, 128)
        tile = flux_x - moved_x + flux_y - pltpu.roll(flux_y, 1, axis=1)
        out[:, pl.ds(pl.multiple_of(l * BY, BY), BY), :] = tile
        return carry

    lax.fori_loop(0, bricks, finish, 0)


def radix_forward(f):
    e = [f[a] + f[a + 8] for a in range(8)]
    o = [f[a] - f[a + 8] for a in range(8)]
    p = [e[a] + e[a + 4] for a in range(4)]
    q = [e[a] - e[a + 4] for a in range(4)]
    even, odd = p[0] + p[2], p[1] + p[3]
    out = [None] * 8
    out[0] = (even + odd, even - odd)
    out[4] = (p[0] - p[2], p[3] - p[1])
    t1 = C2 * (q[1] - q[3])
    t2 = C2 * (q[1] + q[3])
    out[2] = (q[0] + t1, -(q[2] + t2))
    out[6] = (q[0] - t1, q[2] - t2)
    d = [None] + [o[a] - o[8 - a] for a in range(1, 4)]
    s = [None] + [o[a] + o[8 - a] for a in range(1, 4)]
    d2, s2 = C2 * d[2], C2 * s[2]
    base_p, base_m = o[0] + d2, o[0] - d2
    u1 = C1 * d[1] + C3 * d[3]
    u3 = C3 * d[1] - C1 * d[3]
    v1 = C3 * s[1] + C1 * s[3]
    v3 = C1 * s[1] - C3 * s[3]
    w_p, w_m = s2 + o[4], s2 - o[4]
    out[1] = (base_p + u1, -(v1 + w_p))
    out[7] = (base_p - u1, w_p - v1)
    out[3] = (base_m + u3, -(v3 + w_m))
    out[5] = (base_m - u3, w_m - v3)
    return out


def radix_inverse(h):
    (h0, h8) = h[0]
    plus, minus = h0 + h8, h0 - h8
    r4, i4 = h[4]
    part_a = [plus + r4, minus - i4, plus - r4, minus + i4]
    (r2, i2), (r6, i6) = h[2], h[6]
    dr, sr = r2 - r6, r2 + r6
    di, si = i2 - i6, i2 + i6
    part_b = [sr, C2 * (dr - si), -di, -C2 * (dr + si)]
    e = [part_a[a] + part_b[a] for a in range(4)] + [part_a[a] - part_b[a] for a in range(4)]
    (r1, i1), (r3, i3), (r5, i5), (r7, i7) = h[1], h[3], h[5], h[7]
    p17, m17, p35, m35 = r1 + r7, r1 - r7, r3 + r5, r3 - r5
    sums = [p17 + p35, C1 * m17 + C3 * m35, C2 * (p17 - p35), C3 * m17 - C1 * m35]
    ip17, im17, ip35, im35 = i1 + i7, i1 - i7, i3 + i5, i3 - i5
    q1 = C3 * ip17 + C1 * ip35
    q2 = C2 * (im17 + im35)
    q3 = C1 * ip17 - C3 * ip35
    q4 = im17 - im35
    o = [
        sums[0],
        sums[1] - q1,
        sums[2] - q2,
        sums[3] - q3,
        -q4,
        -sums[3] - q3,
        -sums[2] - q2,
        -sums[1] - q1,
    ]
    return [e[a] + o[a] for a in range(8)] + [e[a] - o[a] for a in range(8)]


def forward_kernel(f, fh, fm, fl, ss, s2, edges, resp, nyq, wave, out_edge, xp, xl):
    step = 16

    def radix(t, carry):
        rows = pl.ds(pl.multiple_of(t * step, step), step)
        far_rows = pl.ds(pl.multiple_of(128 + t * step, step), step)
        parts = radix_forward([f[a, rows, :] for a in range(16)])
        for slot in range(SLOTS):
            for where, value in ((rows, parts[slot][0]), (far_rows, parts[slot][1])):
                high, mid, low = split3(value)
                xp[slot, where, 0:128] = high
                xp[slot, where, 128:256] = mid
                xl[slot, where, :] = low
        return carry

    lax.fori_loop(0, 128 // step, radix, 0)

    def solve(s, carry):
        both = xp[s]
        wide = dot(fh[s], both) + dot(fm[s], both)
        spec = wide[:, 0:128] + wide[:, 128:256]
        spec += dot(fh[s], xl[s]) + dot(fl[s], both[:, 0:128])
        high, mid, low = split3(spec)
        wide = dot(jnp.concatenate([high, mid], axis=1), ss[...])
        bent = wide[:, 0:128] + wide[:, 128:256]
        bent += dot(jnp.concatenate([high, low], axis=1), s2[...])
        wave[s] = bent
        high, mid, low = split3(bent * resp[s])
        many = jnp.concatenate([high, mid, high, mid, low, high], axis=1)
        ends = lax.dot_general(
            edges[...], many, (((1,), (1,)), ((), ())), preferred_element_type=F32
        )
        total = ends[2:3] + (ends[0:1] - ends[1:2]) * nyq[s]
        piece = jnp.concatenate([ends[0:2], total, total], axis=0)
        for e in range(GX):
            out_edge[e, s] = piece
        return carry

    lax.fori_loop(0, SLOTS, solve, 0)


def backward_kernel(me, wave, ends, link0, link1, resp, ranks, back1, back2, ih, im, ind, grad, hs):
    row = lax.broadcasted_iota(jnp.int32, (4, 256), 0)

    def solve(s, carry):
        total = jnp.zeros((4, 256), F32)
        alternate = jnp.zeros((1, 256), F32)
        for e in range(GX):
            n = (me[0] - e + GX) % GX
            piece = ends[e, s]
            total += link0[n, s] * piece[0:1] + link1[n, s] * piece[1:2]
            alternate += piece[2:3]
        total = jnp.where(row == 2, alternate * (1.0 / NX), total)
        high, mid = split2(total)
        left = jnp.concatenate([high, mid, high, jnp.zeros_like(high)], axis=0)
        wide = lax.dot_general(left, ranks[...], (((0,), (0,)), ((), ())), preferred_element_type=F32)
        bent = resp[s] * (wave[s] - wide[:, 0:128]) - wide[:, 128:256]
        high, mid = split2(bent)
        line = dot(jnp.concatenate([high, mid], axis=1), back1[...]) + dot(high, back2[...])
        line = jnp.concatenate([line[:, 0:128], line[:, 128:256] + wide[:, 256:384]], axis=1)
        high, mid = split2(line)
        hs[s] = dot(ih[s], high) + dot(ih[s], mid) + dot(im[s], high)
        return carry

    lax.fori_loop(0, SLOTS, solve, 0)
    step = 8

    def radix(t, carry):
        rows = pl.ds(pl.multiple_of(t * step, step), step)
        far_rows = pl.ds(pl.multiple_of(128 + t * step, step), step)
        for part in range(2):
            lanes = slice(128 * part, 128 * part + 128)
            values = radix_inverse([(hs[s, rows, lanes], hs[s, far_rows, lanes]) for s in range(SLOTS)])
            for a in range(16):
                where = pl.ds(pl.multiple_of(a * 128 + t * step, step), step)
                if part == 0:
                    ind[where, :] = values[a]
                else:
                    grad[0, where, :] = values[a]
        return carry

    lax.fori_loop(0, 128 // step, radix, 0)
    grad[1, 0 : NY - 1, :] = ind[1:NY, :] - ind[0 : NY - 1, :]
    grad[1, NY - 1 : NY, :] = ind[0:1, :] - ind[NY - 1 : NY, :]


def vmem():
    return pl.BlockSpec(memory_space=pltpu.VMEM)


def smem():
    return pl.BlockSpec(memory_space=pltpu.SMEM)


def params():
    return pltpu.CompilerParams(vmem_limit_bytes=56 * 1024 * 1024)


def pack(owner, brick, fill, normals, fractions, offsets):
    return pl.pallas_call(
        pack_kernel,
        out_shape=jax.ShapeDtypeStruct((DEV, 5, 4, 128), F32),
        in_specs=[smem()] * 3 + [vmem()] * 3,
        out_specs=vmem(),
        scratch_shapes=[pltpu.SMEM((DEV,), jnp.int32)],
        compiler_params=params(),
        interpret=INTERPRET,
        name="pack",
    )(owner, brick, fill, normals, fractions, offsets)


def splat(first, recv):
    return pl.pallas_call(
        splat_kernel,
        out_shape=jax.ShapeDtypeStruct((Z, NY // GY, 128), F32),
        in_specs=[smem(), vmem()],
        out_specs=vmem(),
        scratch_shapes=[pltpu.VMEM((32, 192, 128), F32)],
        compiler_params=params(),
        interpret=INTERPRET,
        name="splat",
    )(first, recv)


def forward(f):
    t = tables()
    return pl.pallas_call(
        forward_kernel,
        out_shape=(
            jax.ShapeDtypeStruct((SLOTS, 256, 128), F32),
            jax.ShapeDtypeStruct((GX, SLOTS, 4, 256), F32),
        ),
        in_specs=[vmem()] * 9,
        out_specs=(vmem(), vmem()),
        scratch_shapes=[pltpu.VMEM((SLOTS, 256, 256), BF16), pltpu.VMEM((SLOTS, 256, 128), BF16)],
        compiler_params=params(),
        interpret=INTERPRET,
        name="forward",
    )(f, t["fh"], t["fm"], t["fl"], t["ss"], t["s2"], t["edges"], t["resp"], t["nyq"])


def backward(me, wave, ends):
    t = tables()
    return pl.pallas_call(
        backward_kernel,
        out_shape=(
            jax.ShapeDtypeStruct((NY, 128), F32),
            jax.ShapeDtypeStruct((2, NY, 128), F32),
        ),
        in_specs=[smem()] + [vmem()] * 10,
        out_specs=(vmem(), vmem()),
        scratch_shapes=[pltpu.VMEM((SLOTS, 256, 256), F32)],
        compiler_params=params(),
        interpret=INTERPRET,
        name="backward",
    )(
        me, wave, ends, t["link0"], t["link1"], t["resp"], t["ranks"], t["back1"], t["back2"],
        t["ih"], t["im"],
    )


def shards(normals, fractions, offsets, owner, brick, fill):
    send = pack(owner[:, 0], brick, fill, normals, fractions, offsets)
    recv = lax.all_to_all(send, ("gx", "gy"), split_axis=0, concat_axis=0, tiled=True)
    first = recv[:, 4, 0::2, 0].astype(jnp.int32).reshape(2 * DEV)
    tile = splat(first, recv)
    plane = lax.all_to_all(tile, "gy", split_axis=0, concat_axis=0, tiled=True)
    wave, edge = forward(plane.reshape(16, 128, 128))
    ends = lax.all_to_all(edge, "gx", split_axis=0, concat_axis=0, tiled=True)
    me = lax.axis_index("gx").astype(jnp.int32).reshape(1)
    ind, grad = backward(me, wave, ends)
    return ind[None], grad[:, None]


def solution(mesh):
    in_specs = (
        P(("gx", "gy"), None, None),
        P(("gx", "gy"), None, None),
        P(("gx", "gy"), None),
        P(("gx", "gy"), None),
        P(("gx", "gy")),
        P(("gx", "gy")),
    )
    out_specs = (P("gy", None, "gx"), P(None, "gy", None, "gx"))
    return jax.shard_map(shards, mesh=mesh, in_specs=in_specs, out_specs=out_specs, check_vma=False)
```

```python
import functools
import math

import jax
import jax.numpy as jnp
import numpy as np
from jax import lax
from jax.experimental import pallas as pl
from jax.experimental.pallas import tpu as pltpu
from jax.sharding import PartitionSpec as P

NX = 2048
NY = 2048
Z = 8
BX = 128
BY = 8
P_SIZE = 256
GX = 16
GY = 8
DEV = GX * GY
ALPHA = 4e-06
SLOTS = 8
F32 = jnp.float32
BF16 = jnp.bfloat16
C1 = math.cos(math.pi / 8)
C2 = math.cos(math.pi / 4)
C3 = math.cos(3 * math.pi / 8)
INTERPRET = False
SPLAT_UNROLL = 16
SLOT_UNROLL = 8
RADIX_UNROLL = 2


def np_split(values, parts):
    pieces = []
    rest = np.asarray(values, np.float64)
    for _ in range(parts):
        piece = rest.astype(BF16)
        pieces.append(piece)
        rest = rest - piece.astype(np.float64)
    return pieces


def slot_rows():
    ky = np.zeros((SLOTS, 256), np.int64)
    k2 = np.arange(128)
    half = np.arange(64)
    ky[0] = np.concatenate([16 * half, 16 * half, 8 + 16 * half, 8 + 16 * half])
    for slot in range(1, SLOTS):
        ky[slot] = np.concatenate([slot + 16 * k2, slot + 16 * k2])
    return ky


@functools.lru_cache(None)
def tables():
    ky = slot_rows()
    b = np.arange(128)
    fwd = np.zeros((SLOTS, 256, 256))
    weight = np.full((SLOTS, 256), 2.0 / NY)
    half = np.arange(64)
    for part in range(2):
        freq = part * 8 + 16 * half
        theta = 2 * np.pi * ((freq[:, None] * b[None, :]) % NY) / NY
        fwd[0, part * 128 : part * 128 + 64, part * 128 : part * 128 + 128] = np.cos(theta)
        fwd[0, part * 128 + 64 : part * 128 + 128, part * 128 : part * 128 + 128] = -np.sin(theta)
    weight[0, 0] = 1.0 / NY
    for slot in range(1, SLOTS):
        freq = slot + 16 * np.arange(128)
        theta = 2 * np.pi * ((freq[:, None] * b[None, :]) % NY) / NY
        cos, sin = np.cos(theta), np.sin(theta)
        fwd[slot] = np.block([[cos, sin], [-sin, cos]])
    inv = np.transpose(fwd, (0, 2, 1)) * weight[:, None, :]
    c = 4 * np.sin(np.pi * np.minimum(ky, NY - ky) / NY) ** 2 + ALPHA
    j = np.arange(1, 129)
    mu = 4 * np.sin(np.pi * j / 258) ** 2
    resp = -1.0 / (mu[None, None, :] + c[:, :, None])
    x = np.arange(128)
    sine = np.sqrt(2 / 129) * np.sin(np.pi * (x[:, None] + 1) * j[None, :] / 129)
    alt = ((-1.0) ** x) @ sine
    edge = np.zeros((8, 128))
    edge[0], edge[1], edge[2] = sine[0], sine[127], alt
    nyq = 1.0 / (-4.0 - c)
    root = np.sqrt(c * (c + 4))
    big = 1 + c / 2 + root / 2
    logr = -np.log(big)

    def green(n):
        n = n % NX
        return -(np.exp(logr * n) + np.exp(logr * (NX - n))) / (root * (1 - np.exp(logr * NX)))

    link0 = np.zeros((GX, SLOTS, 4, 256))
    link1 = np.zeros((GX, SLOTS, 4, 256))
    for n in range(GX):
        link0[n, :, 0] = -green(128 * n)
        link1[n, :, 0] = -green(128 * (n - 1) - 1) + (1.0 if n == 1 else 0.0)
        link0[n, :, 1] = -green(128 * (n + 1) + 1) + (1.0 if n == GX - 1 else 0.0)
        link1[n, :, 1] = -green(128 * n)
    fh, fm, fl = np_split(fwd, 3)
    ih, im = np_split(inv, 2)
    sh, sm, sl = np_split(sine, 3)
    ss = np.block([[sh, sm], [sh, sm]])
    s2 = np.concatenate([sl, sh], axis=0)
    eh, em, el = np_split(edge, 3)
    edges = np.concatenate([eh, eh, em, em, eh, el], axis=1)
    diff = np.concatenate([sine[:, 1:], np.zeros((128, 1))], axis=1) - sine
    back = np.concatenate([sine.T, np.concatenate([sine.T[:, 1:], np.zeros((128, 1))], axis=1) - sine.T], axis=1)
    bh, bm = np_split(back, 2)
    back1 = np.concatenate([bh, bh], axis=0)
    rank = np.zeros((4, 384))
    rank[0, 0:128] = sine[0]
    rank[1, 0:128] = sine[127]
    rank[2, 128:256] = alt
    rank[1, 256 + 127] = 1.0
    rank[2, 256 + 127] = -1.0
    rh, rm = np_split(rank, 2)
    ranks = np.concatenate([rh, rh, rm, np.zeros((4, 384), BF16)], axis=0)
    f = np.float32
    return dict(
        fh=fh, fm=fm, fl=fl, ih=ih, im=im, ss=ss, s2=s2, edges=edges, resp=resp.astype(f),
        nyq=nyq.reshape(SLOTS, 1, 256).astype(f), link0=link0.astype(f), link1=link1.astype(f),
        back1=back1, back2=bm, ranks=ranks,
    )


def split2(value):
    high = value.astype(BF16)
    return high, (value - high.astype(F32)).astype(BF16)


def split3(value):
    high = value.astype(BF16)
    rest = value - high.astype(F32)
    mid = rest.astype(BF16)
    return high, mid, (rest - mid.astype(F32)).astype(BF16)


def dot(left, right):
    return jnp.dot(left, right, preferred_element_type=F32)


def pack_kernel(owner, brick, fill, normals, fractions, offsets, send, counts):
    blocks = normals.shape[0]

    def clear(d, carry):
        counts[d] = 0
        send[d, 4] = jnp.full((4, 128), -1.0, F32)
        return carry

    lax.fori_loop(0, DEV, clear, 0, unroll=8)
    lane = lax.broadcasted_iota(jnp.int32, (2, 256), 1)
    row4 = lax.broadcasted_iota(jnp.int32, (4, 128), 0)

    def one(b, carry):
        d = owner[b]
        slot = counts[d]
        counts[d] = slot + 1
        live = jnp.where(lane < fill[b], normals[b], 0.0)
        frac = fractions[b]
        send[d, 2 * slot] = jnp.concatenate([live[:, :128], live[:, 128:]], axis=0)
        send[d, 2 * slot + 1] = jnp.concatenate(
            [frac[1:2, :128], frac[0:1, :128], frac[1:2, 128:], frac[0:1, 128:]], axis=0
        )
        cell = (offsets[pl.ds(b, 1), :] + brick[b] * (Z * BY * BX)).astype(F32)
        two = jnp.concatenate([cell[:, :128], cell[:, 128:]], axis=0)
        send[d, 4] = jnp.where(row4 // 2 == slot, jnp.concatenate([two, two], axis=0), send[d, 4])
        return carry

    lax.fori_loop(0, blocks, one, 0, unroll=4)


def splat_kernel(recv, out, acc):
    bricks = acc.shape[0]

    def clear(l, carry):
        acc[l] = jnp.zeros(acc.shape[1:], F32)
        return carry

    lax.fori_loop(0, bricks, clear, 0)
    rows = lax.broadcasted_iota(jnp.int32, (32, 128), 0).astype(F32).astype(BF16)
    cols = lax.broadcasted_iota(jnp.int32, (256, 128), 0).astype(F32).astype(BF16)
    zero = jnp.zeros((), BF16)
    one_b = jnp.ones((), BF16)

    def spread(row, count):
        tile = jnp.broadcast_to(row, (16, 128)).astype(BF16)
        return jnp.concatenate([tile] * (count // 16), axis=0)

    def build(d, slot):
        cell2 = recv[d, 4][2 * slot : 2 * slot + 2].astype(jnp.int32)
        filled = cell2[0:1] >= 0
        norm = jnp.where(filled, recv[d, 2 * slot], 0.0)
        frac = jnp.where(filled, recv[d, 2 * slot + 1], 0.0)
        far = norm * frac
        near = norm * (1.0 - frac)
        near_h = near.astype(BF16).astype(F32)
        far_h = far.astype(BF16).astype(F32)
        near_l = near - near_h
        far_l = far - far_h
        line2 = (((cell2 >> 11) & 3) * 8 + ((cell2 >> 7) & 7)).astype(F32)
        next2 = line2 + 1.0
        col2 = (((cell2 >> 10) & 1) * 128 + (cell2 & 127)).astype(F32)
        left, right = [], []
        for half in range(2):
            here = spread(line2[half : half + 1], 32) == rows
            below = spread(next2[half : half + 1], 32) == rows
            x = 2 * half
            parts = []
            for near_v, far_v in ((near_h, far_h), (near_l, far_l)):
                parts.append(
                    jnp.where(
                        here,
                        spread(near_v[x : x + 1], 32),
                        jnp.where(below, spread(far_v[x : x + 1], 32), zero),
                    )
                )
                parts.append(jnp.where(here, spread(near_v[x + 1 : x + 2], 32), zero))
                parts.append(jnp.where(here, spread(far_v[x + 1 : x + 2], 32), zero))
            left.append(jnp.concatenate(parts, axis=0))
            right.append(jnp.where(spread(col2[half : half + 1], 256) == cols, one_b, zero))
        piece = lax.dot_general(
            jnp.concatenate(left, axis=1),
            jnp.concatenate(right, axis=1),
            (((1,), (1,)), ((), ())),
            preferred_element_type=F32,
        )
        return piece[0:96] + piece[96:192], jnp.maximum(cell2[0, 0] >> 13, 0)

    group = 2 * SPLAT_UNROLL

    def one(i, carry):
        for piece, l in [build(i * SPLAT_UNROLL + k // 2, k % 2) for k in range(group)]:
            acc[l] += piece
        return carry

    lax.fori_loop(0, DEV // SPLAT_UNROLL, one, 0)

    def finish(l, carry):
        for odd in range(2):
            lanes = slice(128 * odd, 128 * odd + 128)
            flux_x = acc[l, 0:32, lanes]
            flux_y = acc[l, 32:64, lanes] + pltpu.roll(acc[l, 64:96, lanes], 1, axis=1)
            moved_x = pltpu.roll(flux_x, 1, axis=1)
            flux_y = flux_y.reshape(4, BY, 128)
            tile = (flux_x - moved_x).reshape(4, BY, 128) + flux_y - pltpu.roll(flux_y, 1, axis=1)
            for plane in range(4):
                out[2 * plane + odd, pl.ds(pl.multiple_of(l * BY, BY), BY), :] = tile[plane]
        return carry

    lax.fori_loop(0, bricks, finish, 0)


def radix_forward(f):
    e = [f[a] + f[a + 8] for a in range(8)]
    o = [f[a] - f[a + 8] for a in range(8)]
    p = [e[a] + e[a + 4] for a in range(4)]
    q = [e[a] - e[a + 4] for a in range(4)]
    even, odd = p[0] + p[2], p[1] + p[3]
    out = [None] * 8
    out[0] = (even + odd, even - odd)
    out[4] = (p[0] - p[2], p[3] - p[1])
    t1 = C2 * (q[1] - q[3])
    t2 = C2 * (q[1] + q[3])
    out[2] = (q[0] + t1, -(q[2] + t2))
    out[6] = (q[0] - t1, q[2] - t2)
    d = [None] + [o[a] - o[8 - a] for a in range(1, 4)]
    s = [None] + [o[a] + o[8 - a] for a in range(1, 4)]
    d2, s2 = C2 * d[2], C2 * s[2]
    base_p, base_m = o[0] + d2, o[0] - d2
    u1 = C1 * d[1] + C3 * d[3]
    u3 = C3 * d[1] - C1 * d[3]
    v1 = C3 * s[1] + C1 * s[3]
    v3 = C1 * s[1] - C3 * s[3]
    w_p, w_m = s2 + o[4], s2 - o[4]
    out[1] = (base_p + u1, -(v1 + w_p))
    out[7] = (base_p - u1, w_p - v1)
    out[3] = (base_m + u3, -(v3 + w_m))
    out[5] = (base_m - u3, w_m - v3)
    return out


def radix_inverse(h):
    (h0, h8) = h[0]
    plus, minus = h0 + h8, h0 - h8
    r4, i4 = h[4]
    part_a = [plus + r4, minus - i4, plus - r4, minus + i4]
    (r2, i2), (r6, i6) = h[2], h[6]
    dr, sr = r2 - r6, r2 + r6
    di, si = i2 - i6, i2 + i6
    part_b = [sr, C2 * (dr - si), -di, -C2 * (dr + si)]
    e = [part_a[a] + part_b[a] for a in range(4)] + [part_a[a] - part_b[a] for a in range(4)]
    (r1, i1), (r3, i3), (r5, i5), (r7, i7) = h[1], h[3], h[5], h[7]
    p17, m17, p35, m35 = r1 + r7, r1 - r7, r3 + r5, r3 - r5
    sums = [p17 + p35, C1 * m17 + C3 * m35, C2 * (p17 - p35), C3 * m17 - C1 * m35]
    ip17, im17, ip35, im35 = i1 + i7, i1 - i7, i3 + i5, i3 - i5
    q1 = C3 * ip17 + C1 * ip35
    q2 = C2 * (im17 + im35)
    q3 = C1 * ip17 - C3 * ip35
    q4 = im17 - im35
    o = [
        sums[0],
        sums[1] - q1,
        sums[2] - q2,
        sums[3] - q3,
        -q4,
        -sums[3] - q3,
        -sums[2] - q2,
        -sums[1] - q1,
    ]
    return [e[a] + o[a] for a in range(8)] + [e[a] - o[a] for a in range(8)]


def forward_kernel(f, fh, fm, fl, ss, s2, edges, resp, nyq, wave, out_edge, xp, xl):
    step = 16

    def radix(t, carry):
        rows = pl.ds(pl.multiple_of(t * step, step), step)
        far_rows = pl.ds(pl.multiple_of(128 + t * step, step), step)
        parts = radix_forward([f[a, rows, :] for a in range(16)])
        for slot in range(SLOTS):
            for where, value in ((rows, parts[slot][0]), (far_rows, parts[slot][1])):
                high, mid, low = split3(value)
                xp[slot, where, 0:128] = high
                xp[slot, where, 128:256] = mid
                xl[slot, where, :] = low
        return carry

    lax.fori_loop(0, 128 // step, radix, 0, unroll=RADIX_UNROLL)

    def solve(s, carry):
        both = xp[s]
        wide = dot(fh[s], both) + dot(fm[s], both)
        spec = wide[:, 0:128] + wide[:, 128:256]
        spec += dot(fh[s], xl[s]) + dot(fl[s], both[:, 0:128])
        high, mid, low = split3(spec)
        wide = dot(jnp.concatenate([high, mid], axis=1), ss[...])
        bent = wide[:, 0:128] + wide[:, 128:256]
        bent += dot(jnp.concatenate([high, low], axis=1), s2[...])
        wave[s] = bent
        high, mid, low = split3(bent * resp[s])
        many = jnp.concatenate([high, mid, high, mid, low, high], axis=1)
        ends = lax.dot_general(
            edges[...], many, (((1,), (1,)), ((), ())), preferred_element_type=F32
        )
        total = ends[2:3] + (ends[0:1] - ends[1:2]) * nyq[s]
        piece = jnp.concatenate([ends[0:2], total, total], axis=0)
        for e in range(GX):
            out_edge[e, s] = piece
        return carry

    lax.fori_loop(0, SLOTS, solve, 0, unroll=SLOT_UNROLL)


def backward_kernel(me, wave, ends, link0, link1, resp, ranks, back1, back2, ih, im, ind, grad, hs):
    row = lax.broadcasted_iota(jnp.int32, (4, 256), 0)

    def solve(s, carry):
        total = jnp.zeros((4, 256), F32)
        alternate = jnp.zeros((1, 256), F32)
        for e in range(GX):
            n = (me[0] - e + GX) % GX
            piece = ends[e, s]
            total += link0[n, s] * piece[0:1] + link1[n, s] * piece[1:2]
            alternate += piece[2:3]
        total = jnp.where(row == 2, alternate * (1.0 / NX), total)
        high, mid = split2(total)
        left = jnp.concatenate([high, mid, high, jnp.zeros_like(high)], axis=0)
        wide = lax.dot_general(left, ranks[...], (((0,), (0,)), ((), ())), preferred_element_type=F32)
        bent = resp[s] * (wave[s] - wide[:, 0:128]) - wide[:, 128:256]
        high, mid = split2(bent)
        line = dot(jnp.concatenate([high, mid], axis=1), back1[...]) + dot(high, back2[...])
        line = jnp.concatenate([line[:, 0:128], line[:, 128:256] + wide[:, 256:384]], axis=1)
        high, mid = split2(line)
        hs[s] = dot(ih[s], high) + dot(ih[s], mid) + dot(im[s], high)
        return carry

    lax.fori_loop(0, SLOTS, solve, 0, unroll=SLOT_UNROLL)
    step = 8

    def radix(t, carry):
        rows = pl.ds(pl.multiple_of(t * step, step), step)
        far_rows = pl.ds(pl.multiple_of(128 + t * step, step), step)
        for part in range(2):
            lanes = slice(128 * part, 128 * part + 128)
            values = radix_inverse([(hs[s, rows, lanes], hs[s, far_rows, lanes]) for s in range(SLOTS)])
            for a in range(16):
                where = pl.ds(pl.multiple_of(a * 128 + t * step, step), step)
                if part == 0:
                    ind[where, :] = values[a]
                else:
                    grad[0, where, :] = values[a]
        return carry

    lax.fori_loop(0, 128 // step, radix, 0, unroll=RADIX_UNROLL)
    grad[1, 0 : NY - 1, :] = ind[1:NY, :] - ind[0 : NY - 1, :]
    grad[1, NY - 1 : NY, :] = ind[0:1, :] - ind[NY - 1 : NY, :]


def vmem():
    return pl.BlockSpec(memory_space=pltpu.VMEM)


def smem():
    return pl.BlockSpec(memory_space=pltpu.SMEM)


def params(mib):
    return pltpu.CompilerParams(vmem_limit_bytes=mib * 1024 * 1024)


def pack(owner, brick, fill, normals, fractions, offsets):
    return pl.pallas_call(
        pack_kernel,
        out_shape=jax.ShapeDtypeStruct((DEV, 5, 4, 128), F32),
        in_specs=[smem()] * 3 + [vmem()] * 3,
        out_specs=vmem(),
        scratch_shapes=[pltpu.SMEM((DEV,), jnp.int32)],
        compiler_params=params(6),
        interpret=INTERPRET,
        name="pack",
    )(owner, brick, fill, normals, fractions, offsets)


def splat(recv):
    return pl.pallas_call(
        splat_kernel,
        out_shape=jax.ShapeDtypeStruct((Z, NY // GY, 128), F32),
        in_specs=[vmem()],
        out_specs=vmem(),
        scratch_shapes=[pltpu.VMEM((32, 96, 256), F32)],
        compiler_params=params(12),
        interpret=INTERPRET,
        name="splat",
    )(recv)


def forward(f):
    t = tables()
    return pl.pallas_call(
        forward_kernel,
        out_shape=(
            jax.ShapeDtypeStruct((SLOTS, 256, 128), F32),
            jax.ShapeDtypeStruct((GX, SLOTS, 4, 256), F32),
        ),
        in_specs=[vmem()] * 9,
        out_specs=(vmem(), vmem()),
        scratch_shapes=[pltpu.VMEM((SLOTS, 256, 256), BF16), pltpu.VMEM((SLOTS, 256, 128), BF16)],
        compiler_params=params(16),
        interpret=INTERPRET,
        name="forward",
    )(f, t["fh"], t["fm"], t["fl"], t["ss"], t["s2"], t["edges"], t["resp"], t["nyq"])


def backward(me, wave, ends):
    t = tables()
    return pl.pallas_call(
        backward_kernel,
        out_shape=(
            jax.ShapeDtypeStruct((NY, 128), F32),
            jax.ShapeDtypeStruct((2, NY, 128), F32),
        ),
        in_specs=[smem()] + [vmem()] * 10,
        out_specs=(vmem(), vmem()),
        scratch_shapes=[pltpu.VMEM((SLOTS, 256, 256), F32)],
        compiler_params=params(16),
        interpret=INTERPRET,
        name="backward",
    )(
        me, wave, ends, t["link0"], t["link1"], t["resp"], t["ranks"], t["back1"], t["back2"],
        t["ih"], t["im"],
    )


def shards(normals, fractions, offsets, owner, brick, fill):
    send = pack(owner[:, 0], brick, fill, normals, fractions, offsets)
    recv = lax.all_to_all(send, ("gx", "gy"), split_axis=0, concat_axis=0, tiled=True)
    tile = splat(recv)
    plane = lax.all_to_all(tile, "gy", split_axis=0, concat_axis=0, tiled=True)
    wave, edge = forward(plane.reshape(16, 128, 128))
    ends = lax.all_to_all(edge, "gx", split_axis=0, concat_axis=0, tiled=True)
    me = lax.axis_index("gx").astype(jnp.int32).reshape(1)
    ind, grad = backward(me, wave, ends)
    return ind[None], grad[:, None]


def solution(mesh):
    in_specs = (
        P(("gx", "gy"), None, None),
        P(("gx", "gy"), None, None),
        P(("gx", "gy"), None),
        P(("gx", "gy"), None),
        P(("gx", "gy")),
        P(("gx", "gy")),
    )
    out_specs = (P("gy", None, "gx"), P(None, "gy", None, "gx"))
    return jax.shard_map(shards, mesh=mesh, in_specs=in_specs, out_specs=out_specs, check_vma=False)
```

```python
import functools
import math

import jax
import jax.numpy as jnp
import numpy as np
from jax import lax
from jax.experimental import pallas as pl
from jax.experimental.pallas import tpu as pltpu
from jax.sharding import PartitionSpec as P

NX = 2048
NY = 2048
Z = 8
BX = 128
BY = 8
P_SIZE = 256
GX = 16
GY = 8
DEV = GX * GY
ALPHA = 4e-06
SLOTS = 8
F32 = jnp.float32
BF16 = jnp.bfloat16
C1 = math.cos(math.pi / 8)
C2 = math.cos(math.pi / 4)
C3 = math.cos(3 * math.pi / 8)
INTERPRET = False
SPLAT_UNROLL = 16
RADIX_UNROLL = 2
LF = 24
LB = 50


def np_split(values, parts):
    pieces = []
    rest = np.asarray(values, np.float64)
    for _ in range(parts):
        piece = rest.astype(BF16)
        pieces.append(piece)
        rest = rest - piece.astype(np.float64)
    return pieces


def slot_rows():
    ky = np.zeros((SLOTS, 256), np.int64)
    k2 = np.arange(128)
    half = np.arange(64)
    ky[0] = np.concatenate([16 * half, 16 * half, 8 + 16 * half, 8 + 16 * half])
    for slot in range(1, SLOTS):
        ky[slot] = np.concatenate([slot + 16 * k2, slot + 16 * k2])
    return ky


@functools.lru_cache(None)
def tables():
    ky = slot_rows()
    b = np.arange(128)
    fwd = np.zeros((SLOTS, 256, 256))
    weight = np.full((SLOTS, 256), 2.0 / NY)
    half = np.arange(64)
    for part in range(2):
        freq = part * 8 + 16 * half
        theta = 2 * np.pi * ((freq[:, None] * b[None, :]) % NY) / NY
        fwd[0, part * 128 : part * 128 + 64, part * 128 : part * 128 + 128] = np.cos(theta)
        fwd[0, part * 128 + 64 : part * 128 + 128, part * 128 : part * 128 + 128] = -np.sin(theta)
    weight[0, 0] = 1.0 / NY
    for slot in range(1, SLOTS):
        freq = slot + 16 * np.arange(128)
        theta = 2 * np.pi * ((freq[:, None] * b[None, :]) % NY) / NY
        cos, sin = np.cos(theta), np.sin(theta)
        fwd[slot] = np.block([[cos, sin], [-sin, cos]])
    inv = np.transpose(fwd, (0, 2, 1)) * weight[:, None, :]
    c = 4 * np.sin(np.pi * np.minimum(ky, NY - ky) / NY) ** 2 + ALPHA
    j = np.arange(1, 129)
    mu = 4 * np.sin(np.pi * j / 258) ** 2
    resp = -1.0 / (mu[None, None, :] + c[:, :, None])
    x = np.arange(128)
    sine = np.sqrt(2 / 129) * np.sin(np.pi * (x[:, None] + 1) * j[None, :] / 129)
    alt = ((-1.0) ** x) @ sine
    edge = np.zeros((8, 128))
    edge[0], edge[1], edge[2] = sine[0], sine[127], alt
    nyq = 1.0 / (-4.0 - c)
    root = np.sqrt(c * (c + 4))
    big = 1 + c / 2 + root / 2
    logr = -np.log(big)

    def green(n):
        n = n % NX
        return -(np.exp(logr * n) + np.exp(logr * (NX - n))) / (root * (1 - np.exp(logr * NX)))

    link = np.zeros((2, GX, SLOTS, 256))
    for n in range(GX):
        link[0, n] = -green(128 * n)
        link[1, n] = -green(128 * (n + 1) + 1) + (1.0 if n == GX - 1 else 0.0)
    fh, fm, fl = np_split(fwd, 3)
    ih, im = np_split(inv, 2)
    sh, sm, sl = np_split(sine, 3)
    ss = np.block([[sh, sm], [sh, sm]])
    s2 = np.concatenate([sl, sh], axis=0)
    eh, em = np_split(edge, 2)
    edges = np.block([[eh, eh], [em, em]])
    back = np.concatenate([sine.T, np.concatenate([sine.T[:, 1:], np.zeros((128, 1))], axis=1) - sine.T], axis=1)
    bh, bm = np_split(back, 2)
    back1 = np.concatenate([bh, bh], axis=0)
    rank = np.zeros((3, 384))
    rank[0, 0:128] = sine[0]
    rank[1, 0:128] = sine[127]
    rank[2, 128:256] = alt
    rank[1, 256 + 127] = 1.0
    rank[2, 256 + 127] = -1.0
    rh, rm = np_split(rank, 2)
    ranks = np.concatenate([rh, rh, rm, np.zeros((7, 384), BF16)], axis=0)
    f = np.float32
    return dict(
        fwd=np.concatenate([fh, fm, fl], axis=1), inv=np.concatenate([ih, im], axis=1), ss=ss, s2=s2,
        edges=edges, resp=resp.astype(f), nyq=nyq.reshape(SLOTS, 1, 256).astype(f),
        link=link.astype(f), back1=back1, back2=bm, ranks=ranks,
    )


def split2(value):
    high = value.astype(BF16)
    return high, (value - high.astype(F32)).astype(BF16)


def split3(value):
    high = value.astype(BF16)
    rest = value - high.astype(F32)
    mid = rest.astype(BF16)
    return high, mid, (rest - mid.astype(F32)).astype(BF16)


def dot(left, right):
    return jnp.dot(left, right, preferred_element_type=F32)


def pack_kernel(owner, brick, fill, normals, fractions, offsets, send, counts):
    blocks = normals.shape[0]

    def clear(d, carry):
        counts[d] = 0
        send[d, 4] = jnp.full((4, 128), -1.0, F32)
        return carry

    lax.fori_loop(0, DEV, clear, 0, unroll=8)
    lane = lax.broadcasted_iota(jnp.int32, (2, 256), 1)
    row4 = lax.broadcasted_iota(jnp.int32, (4, 128), 0)

    def one(b, carry):
        d = owner[b]
        slot = counts[d]
        counts[d] = slot + 1
        live = jnp.where(lane < fill[b], normals[b], 0.0)
        frac = fractions[b]
        send[d, 2 * slot] = jnp.concatenate([live[:, :128], live[:, 128:]], axis=0)
        send[d, 2 * slot + 1] = jnp.concatenate(
            [frac[1:2, :128], frac[0:1, :128], frac[1:2, 128:], frac[0:1, 128:]], axis=0
        )
        cell = (offsets[pl.ds(b, 1), :] + brick[b] * (Z * BY * BX)).astype(F32)
        two = jnp.concatenate([cell[:, :128], cell[:, 128:]], axis=0)
        send[d, 4] = jnp.where(row4 // 2 == slot, jnp.concatenate([two, two], axis=0), send[d, 4])
        return carry

    lax.fori_loop(0, blocks, one, 0, unroll=4)


def splat_kernel(recv, out, acc):
    bricks = acc.shape[0]

    def clear(l, carry):
        acc[l] = jnp.zeros(acc.shape[1:], F32)
        return carry

    lax.fori_loop(0, bricks, clear, 0)
    rows = lax.broadcasted_iota(jnp.int32, (32, 128), 0).astype(F32).astype(BF16)
    cols = lax.broadcasted_iota(jnp.int32, (256, 128), 0).astype(F32).astype(BF16)
    zero = jnp.zeros((), BF16)
    one_b = jnp.ones((), BF16)

    def spread(row, count):
        tile = jnp.broadcast_to(row, (16, 128)).astype(BF16)
        return jnp.concatenate([tile] * (count // 16), axis=0)

    def build(d, slot):
        cell2 = recv[d, 4][2 * slot : 2 * slot + 2].astype(jnp.int32)
        filled = cell2[0:1] >= 0
        norm = jnp.where(filled, recv[d, 2 * slot], 0.0)
        frac = jnp.where(filled, recv[d, 2 * slot + 1], 0.0)
        far = norm * frac
        near = norm * (1.0 - frac)
        near_h = near.astype(BF16).astype(F32)
        far_h = far.astype(BF16).astype(F32)
        near_l = near - near_h
        far_l = far - far_h
        line2 = (((cell2 >> 11) & 3) * 8 + ((cell2 >> 7) & 7)).astype(F32)
        next2 = line2 + 1.0
        col2 = (((cell2 >> 10) & 1) * 128 + (cell2 & 127)).astype(F32)
        left, right = [], []
        for half in range(2):
            here = spread(line2[half : half + 1], 32) == rows
            below = spread(next2[half : half + 1], 32) == rows
            x = 2 * half
            parts = []
            for near_v, far_v in ((near_h, far_h), (near_l, far_l)):
                parts.append(
                    jnp.where(
                        here,
                        spread(near_v[x : x + 1], 32),
                        jnp.where(below, spread(far_v[x : x + 1], 32), zero),
                    )
                )
                parts.append(jnp.where(here, spread(near_v[x + 1 : x + 2], 32), zero))
                parts.append(jnp.where(here, spread(far_v[x + 1 : x + 2], 32), zero))
            left.append(jnp.concatenate(parts, axis=0))
            right.append(jnp.where(spread(col2[half : half + 1], 256) == cols, one_b, zero))
        piece = lax.dot_general(
            jnp.concatenate(left, axis=1),
            jnp.concatenate(right, axis=1),
            (((1,), (1,)), ((), ())),
            preferred_element_type=F32,
        )
        return piece[0:96] + piece[96:192], jnp.maximum(cell2[0, 0] >> 13, 0)

    group = 2 * SPLAT_UNROLL

    def one(i, carry):
        for piece, l in [build(i * SPLAT_UNROLL + k // 2, k % 2) for k in range(group)]:
            acc[l] += piece
        return carry

    lax.fori_loop(0, DEV // SPLAT_UNROLL, one, 0)

    def finish(l, carry):
        for odd in range(2):
            lanes = slice(128 * odd, 128 * odd + 128)
            flux_x = acc[l, 0:32, lanes]
            flux_y = acc[l, 32:64, lanes] + pltpu.roll(acc[l, 64:96, lanes], 1, axis=1)
            moved_x = pltpu.roll(flux_x, 1, axis=1)
            flux_y = flux_y.reshape(4, BY, 128)
            tile = (flux_x - moved_x).reshape(4, BY, 128) + flux_y - pltpu.roll(flux_y, 1, axis=1)
            for plane in range(4):
                out[2 * plane + odd, pl.ds(pl.multiple_of(l * BY, BY), BY), :] = tile[plane]
        return carry

    lax.fori_loop(0, bricks, finish, 0)


def radix_forward(f):
    e = [f[a] + f[a + 8] for a in range(8)]
    o = [f[a] - f[a + 8] for a in range(8)]
    p = [e[a] + e[a + 4] for a in range(4)]
    q = [e[a] - e[a + 4] for a in range(4)]
    even, odd = p[0] + p[2], p[1] + p[3]
    out = [None] * 8
    out[0] = (even + odd, even - odd)
    out[4] = (p[0] - p[2], p[3] - p[1])
    t1 = C2 * (q[1] - q[3])
    t2 = C2 * (q[1] + q[3])
    out[2] = (q[0] + t1, -(q[2] + t2))
    out[6] = (q[0] - t1, q[2] - t2)
    d = [None] + [o[a] - o[8 - a] for a in range(1, 4)]
    s = [None] + [o[a] + o[8 - a] for a in range(1, 4)]
    d2, s2 = C2 * d[2], C2 * s[2]
    base_p, base_m = o[0] + d2, o[0] - d2
    u1 = C1 * d[1] + C3 * d[3]
    u3 = C3 * d[1] - C1 * d[3]
    v1 = C3 * s[1] + C1 * s[3]
    v3 = C1 * s[1] - C3 * s[3]
    w_p, w_m = s2 + o[4], s2 - o[4]
    out[1] = (base_p + u1, -(v1 + w_p))
    out[7] = (base_p - u1, w_p - v1)
    out[3] = (base_m + u3, -(v3 + w_m))
    out[5] = (base_m - u3, w_m - v3)
    return out


def radix_inverse(h):
    (h0, h8) = h[0]
    plus, minus = h0 + h8, h0 - h8
    r4, i4 = h[4]
    part_a = [plus + r4, minus - i4, plus - r4, minus + i4]
    (r2, i2), (r6, i6) = h[2], h[6]
    dr, sr = r2 - r6, r2 + r6
    di, si = i2 - i6, i2 + i6
    part_b = [sr, C2 * (dr - si), -di, -C2 * (dr + si)]
    e = [part_a[a] + part_b[a] for a in range(4)] + [part_a[a] - part_b[a] for a in range(4)]
    (r1, i1), (r3, i3), (r5, i5), (r7, i7) = h[1], h[3], h[5], h[7]
    p17, m17, p35, m35 = r1 + r7, r1 - r7, r3 + r5, r3 - r5
    sums = [p17 + p35, C1 * m17 + C3 * m35, C2 * (p17 - p35), C3 * m17 - C1 * m35]
    ip17, im17, ip35, im35 = i1 + i7, i1 - i7, i3 + i5, i3 - i5
    q1 = C3 * ip17 + C1 * ip35
    q2 = C2 * (im17 + im35)
    q3 = C1 * ip17 - C3 * ip35
    q4 = im17 - im35
    o = [
        sums[0],
        sums[1] - q1,
        sums[2] - q2,
        sums[3] - q3,
        -q4,
        -sums[3] - q3,
        -sums[2] - q2,
        -sums[1] - q1,
    ]
    return [e[a] + o[a] for a in range(8)] + [e[a] - o[a] for a in range(8)]


def forward_kernel(f, fwd, ss, s2, edges, resp, nyq, wave, out_edge, xh, xm, xl, ends_all):
    step = 16

    def radix(t, carry):
        rows = pl.ds(pl.multiple_of(t * step, step), step)
        far_rows = pl.ds(pl.multiple_of(128 + t * step, step), step)
        parts = radix_forward([f[a, rows, :] for a in range(16)])
        for slot in range(SLOTS):
            for where, value in ((rows, parts[slot][0]), (far_rows, parts[slot][1])):
                xh[slot, where, :], xm[slot, where, :], xl[slot, where, :] = split3(value)
        return carry

    lax.fori_loop(0, 128 // step, radix, 0, unroll=RADIX_UNROLL)
    for s in range(SLOTS):
        wide = dot(fwd[s], jnp.concatenate([xh[s], xm[s]], axis=1))
        spec = dot(fwd[s, 0:256], xl[s]) + wide[512:768, 0:128]
        spec += wide[256:512, 0:128] + wide[0:256, 128:256] + wide[256:512, 128:256]
        spec += wide[0:256, 0:128]
        high, mid, low = split3(spec)
        wide = dot(jnp.concatenate([high, mid], axis=1), ss[...])
        bent = dot(jnp.concatenate([high, low], axis=1), s2[...])
        bent += wide[:, 128:256] + wide[:, 0:128]
        wave[s] = bent
        high, mid = split2(bent * resp[s])
        ends = lax.dot_general(
            edges[...],
            jnp.concatenate([high, mid], axis=1),
            (((1,), (1,)), ((), ())),
            preferred_element_type=F32,
        )
        ends = ends[0:8] + ends[8:16]
        ends_all[0, s : s + 1] = ends[0:1]
        ends_all[1, s : s + 1] = ends[1:2]
        ends_all[2, s : s + 1] = ends[2:3] + (ends[0:1] - ends[1:2]) * nyq[s]
    for e in range(GX):
        out_edge[e] = ends_all[...]


def backward_kernel(me, wave, ends, link, resp, ranks, back1, back2, inv, ind, grad, hs, invs, sems):
    copies = []
    for s in range(SLOTS):
        copy = pltpu.make_async_copy(inv.at[s], invs.at[s], sems.at[s])
        copy.start()
        copies.append(copy)
    left = jnp.zeros((SLOTS, 256), F32)
    right = jnp.zeros((SLOTS, 256), F32)
    swing = jnp.zeros((SLOTS, 256), F32)
    for e in range(GX):
        n = (me[0] - e + GX) % GX
        first, last = ends[e, 0], ends[e, 1]
        near = link[0, n]
        left += near * first + link[1, (GX - n) % GX] * last
        right += link[1, n] * first + near * last
        swing += ends[e, 2]
    swing *= 1.0 / NX
    values = []
    for value in (left, right, swing):
        high = value.astype(BF16).astype(F32)
        values.append((high, value - high))
    for s in range(SLOTS):
        highs = [high[s : s + 1] for high, _ in values]
        mids = [mid[s : s + 1] for _, mid in values]
        stack = jnp.concatenate(highs + mids + highs + [jnp.zeros((7, 256), F32)], axis=0)
        wide = lax.dot_general(
            stack.astype(BF16), ranks[...], (((0,), (0,)), ((), ())), preferred_element_type=F32
        )
        bent = resp[s] * (wave[s] - wide[:, 0:128]) - wide[:, 128:256]
        high, mid = split2(bent)
        line = dot(jnp.concatenate([high, mid], axis=1), back1[...]) + dot(high, back2[...])
        line = jnp.concatenate([line[:, 0:128], line[:, 128:256] + wide[:, 256:384]], axis=1)
        high, mid = split2(line)
        copies[s].wait()
        wide = dot(invs[s], high)
        hs[s] = dot(invs[s, 0:256], mid) + wide[256:512] + wide[0:256]
    step = 8

    def radix(t, carry):
        rows = pl.ds(pl.multiple_of(t * step, step), step)
        far_rows = pl.ds(pl.multiple_of(128 + t * step, step), step)
        for part in range(2):
            lanes = slice(128 * part, 128 * part + 128)
            values = radix_inverse([(hs[s, rows, lanes], hs[s, far_rows, lanes]) for s in range(SLOTS)])
            for a in range(16):
                where = pl.ds(pl.multiple_of(a * 128 + t * step, step), step)
                if part == 0:
                    ind[where, :] = values[a]
                else:
                    grad[0, where, :] = values[a]
        return carry

    lax.fori_loop(0, 128 // step, radix, 0, unroll=RADIX_UNROLL)
    grad[1, 0 : NY - 1, :] = ind[1:NY, :] - ind[0 : NY - 1, :]
    grad[1, NY - 1 : NY, :] = ind[0:1, :] - ind[NY - 1 : NY, :]


def vmem():
    return pl.BlockSpec(memory_space=pltpu.VMEM)


def smem():
    return pl.BlockSpec(memory_space=pltpu.SMEM)


def params(mib):
    return pltpu.CompilerParams(vmem_limit_bytes=mib * 1024 * 1024)


def pack(owner, brick, fill, normals, fractions, offsets):
    return pl.pallas_call(
        pack_kernel,
        out_shape=jax.ShapeDtypeStruct((DEV, 5, 4, 128), F32),
        in_specs=[smem()] * 3 + [vmem()] * 3,
        out_specs=vmem(),
        scratch_shapes=[pltpu.SMEM((DEV,), jnp.int32)],
        compiler_params=params(56),
        interpret=INTERPRET,
        name="pack",
    )(owner, brick, fill, normals, fractions, offsets)


def splat(recv):
    return pl.pallas_call(
        splat_kernel,
        out_shape=jax.ShapeDtypeStruct((Z, NY // GY, 128), F32),
        in_specs=[vmem()],
        out_specs=vmem(),
        scratch_shapes=[pltpu.VMEM((32, 96, 256), F32)],
        compiler_params=params(12),
        interpret=INTERPRET,
        name="splat",
    )(recv)


def hbm():
    return pl.BlockSpec(memory_space=pltpu.HBM)


def forward(f):
    t = tables()
    return pl.pallas_call(
        forward_kernel,
        out_shape=(
            jax.ShapeDtypeStruct((SLOTS, 256, 128), F32),
            jax.ShapeDtypeStruct((GX, 3, SLOTS, 256), F32),
        ),
        in_specs=[vmem()] * 7,
        out_specs=(vmem(), vmem()),
        scratch_shapes=[pltpu.VMEM((SLOTS, 256, 128), BF16)] * 3
        + [pltpu.VMEM((3, SLOTS, 256), F32)],
        compiler_params=params(LF),
        interpret=INTERPRET,
        name="forward",
    )(f, t["fwd"], t["ss"], t["s2"], t["edges"], t["resp"], t["nyq"])


def backward(me, wave, ends):
    t = tables()
    return pl.pallas_call(
        backward_kernel,
        out_shape=(
            jax.ShapeDtypeStruct((NY, 128), F32),
            jax.ShapeDtypeStruct((2, NY, 128), F32),
        ),
        in_specs=[smem()] + [vmem()] * 7 + [hbm()],
        out_specs=(vmem(), vmem()),
        scratch_shapes=[
            pltpu.VMEM((SLOTS, 256, 256), F32),
            pltpu.VMEM((SLOTS, 512, 256), BF16),
            pltpu.SemaphoreType.DMA((SLOTS,)),
        ],
        compiler_params=params(LB),
        interpret=INTERPRET,
        name="backward",
    )(me, wave, ends, t["link"], t["resp"], t["ranks"], t["back1"], t["back2"], t["inv"])


def shards(normals, fractions, offsets, owner, brick, fill):
    send = pack(owner[:, 0], brick, fill, normals, fractions, offsets)
    recv = lax.all_to_all(send, ("gx", "gy"), split_axis=0, concat_axis=0, tiled=True)
    tile = splat(recv)
    plane = lax.all_to_all(tile, "gy", split_axis=0, concat_axis=0, tiled=True)
    wave, edge = forward(plane.reshape(16, 128, 128))
    ends = lax.all_to_all(edge, "gx", split_axis=0, concat_axis=0, tiled=True)
    me = lax.axis_index("gx").astype(jnp.int32).reshape(1)
    ind, grad = backward(me, wave, ends)
    return ind[None], grad[:, None]


def solution(mesh):
    in_specs = (
        P(("gx", "gy"), None, None),
        P(("gx", "gy"), None, None),
        P(("gx", "gy"), None),
        P(("gx", "gy"), None),
        P(("gx", "gy")),
        P(("gx", "gy")),
    )
    out_specs = (P("gy", None, "gx"), P(None, "gy", None, "gx"))
    return jax.shard_map(shards, mesh=mesh, in_specs=in_specs, out_specs=out_specs, check_vma=False)
```

```python
import functools
import math

import jax
import jax.numpy as jnp
import numpy as np
from jax import lax
from jax.experimental import pallas as pl
from jax.experimental.pallas import tpu as pltpu
from jax.sharding import PartitionSpec as P

NX = 2048
NY = 2048
Z = 8
BX = 128
BY = 8
P_SIZE = 256
GX = 16
GY = 8
DEV = GX * GY
ALPHA = 4e-06
SLOTS = 8
F32 = jnp.float32
BF16 = jnp.bfloat16
C1 = math.cos(math.pi / 8)
C2 = math.cos(math.pi / 4)
C3 = math.cos(3 * math.pi / 8)
INTERPRET = False
SPLAT_UNROLL = 32
FINISH_UNROLL = 8
FGROUP = 8
BGROUP = 4
RADIX_UNROLL = 2
CHUNKS = 4
LF = 24
LB = 51


def np_split(values, parts):
    pieces = []
    rest = np.asarray(values, np.float64)
    for _ in range(parts):
        piece = rest.astype(BF16)
        pieces.append(piece)
        rest = rest - piece.astype(np.float64)
    return pieces


def slot_rows():
    ky = np.zeros((SLOTS, 256), np.int64)
    k2 = np.arange(128)
    half = np.arange(64)
    ky[0] = np.concatenate([16 * half, 16 * half, 8 + 16 * half, 8 + 16 * half])
    for slot in range(1, SLOTS):
        ky[slot] = np.concatenate([slot + 16 * k2, slot + 16 * k2])
    return ky


@functools.lru_cache(None)
def tables():
    ky = slot_rows()
    b = np.arange(128)
    fwd = np.zeros((SLOTS, 256, 256))
    weight = np.full((SLOTS, 256), 2.0 / NY)
    half = np.arange(64)
    for part in range(2):
        freq = part * 8 + 16 * half
        theta = 2 * np.pi * ((freq[:, None] * b[None, :]) % NY) / NY
        fwd[0, part * 128 : part * 128 + 64, part * 128 : part * 128 + 128] = np.cos(theta)
        fwd[0, part * 128 + 64 : part * 128 + 128, part * 128 : part * 128 + 128] = -np.sin(theta)
    weight[0, 0] = 1.0 / NY
    for slot in range(1, SLOTS):
        freq = slot + 16 * np.arange(128)
        theta = 2 * np.pi * ((freq[:, None] * b[None, :]) % NY) / NY
        cos, sin = np.cos(theta), np.sin(theta)
        fwd[slot] = np.block([[cos, sin], [-sin, cos]])
    inv = np.transpose(fwd, (0, 2, 1)) * weight[:, None, :]
    c = 4 * np.sin(np.pi * np.minimum(ky, NY - ky) / NY) ** 2 + ALPHA
    j = np.arange(1, 129)
    mu = 4 * np.sin(np.pi * j / 258) ** 2
    resp = -1.0 / (mu[None, None, :] + c[:, :, None])
    x = np.arange(128)
    sine = np.sqrt(2 / 129) * np.sin(np.pi * (x[:, None] + 1) * j[None, :] / 129)
    alt = ((-1.0) ** x) @ sine
    edge = np.zeros((8, 128))
    edge[0], edge[1], edge[2] = sine[0], sine[127], alt
    nyq = 1.0 / (-4.0 - c)
    root = np.sqrt(c * (c + 4))
    big = 1 + c / 2 + root / 2
    logr = -np.log(big)

    def green(n):
        n = n % NX
        return -(np.exp(logr * n) + np.exp(logr * (NX - n))) / (root * (1 - np.exp(logr * NX)))

    link = np.zeros((2, GX, SLOTS, 256))
    for n in range(GX):
        link[0, n] = -green(128 * n)
        link[1, n] = -green(128 * (n + 1) + 1) + (1.0 if n == GX - 1 else 0.0)
    fh, fm, fl = np_split(fwd, 3)
    ih, im = np_split(inv, 2)
    sh, sm, sl = np_split(sine, 3)
    ss = np.block([[sh, sm], [sh, sm]])
    s2 = np.concatenate([sl, sh], axis=0)
    eh, em = np_split(edge, 2)
    edges = np.block([[eh, eh], [em, em]])
    back = np.concatenate([sine.T, np.concatenate([sine.T[:, 1:], np.zeros((128, 1))], axis=1) - sine.T], axis=1)
    bh, bm = np_split(back, 2)
    back1 = np.concatenate([bh, bh], axis=0)
    rank = np.zeros((3, 384))
    rank[0, 0:128] = sine[0]
    rank[1, 0:128] = sine[127]
    rank[2, 128:256] = alt
    rank[1, 256 + 127] = 1.0
    rank[2, 256 + 127] = -1.0
    rh, rm = np_split(rank, 2)
    ranks = np.concatenate([rh, rh, rm, np.zeros((7, 384), BF16)], axis=0)
    f = np.float32
    return dict(
        fwd=np.concatenate([fh, fm, fl], axis=1), inv=np.concatenate([ih, im], axis=1), ss=ss, s2=s2,
        edges=edges, resp=resp.astype(f), nyq=nyq.reshape(SLOTS, 1, 256).astype(f),
        link=link.astype(f), back1=back1, back2=bm, ranks=ranks,
    )


def split2(value):
    high = value.astype(BF16)
    return high, (value - high.astype(F32)).astype(BF16)


def split3(value):
    high = value.astype(BF16)
    rest = value - high.astype(F32)
    mid = rest.astype(BF16)
    return high, mid, (rest - mid.astype(F32)).astype(BF16)


def dot(left, right):
    return jnp.dot(left, right, preferred_element_type=F32)


def pack_kernel(owner, brick, fill, normals, fractions, offsets, send, counts):
    blocks = normals.shape[0]

    def clear(d, carry):
        counts[d] = 0
        send[d, 4] = jnp.full((4, 128), -1.0, F32)
        return carry

    lax.fori_loop(0, DEV, clear, 0, unroll=8)
    lane = lax.broadcasted_iota(jnp.int32, (2, 256), 1)
    row4 = lax.broadcasted_iota(jnp.int32, (4, 128), 0)

    def one(b, carry):
        d = owner[b]
        slot = counts[d]
        counts[d] = slot + 1
        live = jnp.where(lane < fill[b], normals[b], 0.0)
        frac = fractions[b]
        send[d, 2 * slot] = jnp.concatenate([live[:, :128], live[:, 128:]], axis=0)
        send[d, 2 * slot + 1] = jnp.concatenate(
            [frac[1:2, :128], frac[0:1, :128], frac[1:2, 128:], frac[0:1, 128:]], axis=0
        )
        cell = (offsets[pl.ds(b, 1), :] + brick[b] * (Z * BY * BX)).astype(F32)
        two = jnp.concatenate([cell[:, :128], cell[:, 128:]], axis=0)
        send[d, 4] = jnp.where(row4 // 2 == slot, jnp.concatenate([two, two], axis=0), send[d, 4])
        return carry

    lax.fori_loop(0, blocks, one, 0, unroll=4)


def splat_kernel(recv, out, acc):
    bricks = acc.shape[0]

    def clear(l, carry):
        acc[l] = jnp.zeros(acc.shape[1:], F32)
        return carry

    lax.fori_loop(0, bricks, clear, 0)
    rows = lax.broadcasted_iota(jnp.int32, (32, 128), 0).astype(F32).astype(BF16)
    cols = lax.broadcasted_iota(jnp.int32, (256, 128), 0).astype(F32).astype(BF16)
    zero = jnp.zeros((), BF16)
    one_b = jnp.ones((), BF16)

    def spread(row, count):
        tile = jnp.broadcast_to(row, (16, 128)).astype(BF16)
        return jnp.concatenate([tile] * (count // 16), axis=0)

    def build(d, slot):
        cell2 = recv[d, 4][2 * slot : 2 * slot + 2].astype(jnp.int32)
        filled = cell2[0:1] >= 0
        norm = jnp.where(filled, recv[d, 2 * slot], 0.0)
        frac = jnp.where(filled, recv[d, 2 * slot + 1], 0.0)
        far = norm * frac
        near = norm * (1.0 - frac)
        near_h = near.astype(BF16).astype(F32)
        far_h = far.astype(BF16).astype(F32)
        near_l = near - near_h
        far_l = far - far_h
        line2 = (((cell2 >> 11) & 3) * 8 + ((cell2 >> 7) & 7)).astype(F32)
        next2 = line2 + 1.0
        col2 = (((cell2 >> 10) & 1) * 128 + (cell2 & 127)).astype(F32)
        left, right = [], []
        for half in range(2):
            here = spread(line2[half : half + 1], 32) == rows
            below = spread(next2[half : half + 1], 32) == rows
            x = 2 * half
            parts = []
            for near_v, far_v in ((near_h, far_h), (near_l, far_l)):
                parts.append(
                    jnp.where(
                        here,
                        spread(near_v[x : x + 1], 32),
                        jnp.where(below, spread(far_v[x : x + 1], 32), zero),
                    )
                )
                parts.append(jnp.where(here, spread(near_v[x + 1 : x + 2], 32), zero))
                parts.append(jnp.where(here, spread(far_v[x + 1 : x + 2], 32), zero))
            left.append(jnp.concatenate(parts, axis=0))
            right.append(jnp.where(spread(col2[half : half + 1], 256) == cols, one_b, zero))
        piece = lax.dot_general(
            jnp.concatenate(left, axis=1),
            jnp.concatenate(right, axis=1),
            (((1,), (1,)), ((), ())),
            preferred_element_type=F32,
        )
        return piece[0:96] + piece[96:192], jnp.maximum(cell2[0, 0] >> 13, 0)

    group = 2 * SPLAT_UNROLL

    def one(i, carry):
        for piece, l in [build(i * SPLAT_UNROLL + k // 2, k % 2) for k in range(group)]:
            acc[l] += piece
        return carry

    lax.fori_loop(0, DEV // SPLAT_UNROLL, one, 0)

    def finish(l, carry):
        for odd in range(2):
            lanes = slice(128 * odd, 128 * odd + 128)
            flux_x = acc[l, 0:32, lanes]
            flux_y = acc[l, 32:64, lanes] + pltpu.roll(acc[l, 64:96, lanes], 1, axis=1)
            moved_x = pltpu.roll(flux_x, 1, axis=1)
            flux_y = flux_y.reshape(4, BY, 128)
            tile = (flux_x - moved_x).reshape(4, BY, 128) + flux_y - pltpu.roll(flux_y, 1, axis=1)
            for plane in range(4):
                out[2 * plane + odd, pl.ds(pl.multiple_of(l * BY, BY), BY), :] = tile[plane]
        return carry

    lax.fori_loop(0, bricks, finish, 0, unroll=FINISH_UNROLL)


def radix_forward(f):
    e = [f[a] + f[a + 8] for a in range(8)]
    o = [f[a] - f[a + 8] for a in range(8)]
    p = [e[a] + e[a + 4] for a in range(4)]
    q = [e[a] - e[a + 4] for a in range(4)]
    even, odd = p[0] + p[2], p[1] + p[3]
    out = [None] * 8
    out[0] = (even + odd, even - odd)
    out[4] = (p[0] - p[2], p[3] - p[1])
    t1 = C2 * (q[1] - q[3])
    t2 = C2 * (q[1] + q[3])
    out[2] = (q[0] + t1, -(q[2] + t2))
    out[6] = (q[0] - t1, q[2] - t2)
    d = [None] + [o[a] - o[8 - a] for a in range(1, 4)]
    s = [None] + [o[a] + o[8 - a] for a in range(1, 4)]
    d2, s2 = C2 * d[2], C2 * s[2]
    base_p, base_m = o[0] + d2, o[0] - d2
    u1 = C1 * d[1] + C3 * d[3]
    u3 = C3 * d[1] - C1 * d[3]
    v1 = C3 * s[1] + C1 * s[3]
    v3 = C1 * s[1] - C3 * s[3]
    w_p, w_m = s2 + o[4], s2 - o[4]
    out[1] = (base_p + u1, -(v1 + w_p))
    out[7] = (base_p - u1, w_p - v1)
    out[3] = (base_m + u3, -(v3 + w_m))
    out[5] = (base_m - u3, w_m - v3)
    return out


def radix_inverse(h):
    (h0, h8) = h[0]
    plus, minus = h0 + h8, h0 - h8
    r4, i4 = h[4]
    part_a = [plus + r4, minus - i4, plus - r4, minus + i4]
    (r2, i2), (r6, i6) = h[2], h[6]
    dr, sr = r2 - r6, r2 + r6
    di, si = i2 - i6, i2 + i6
    part_b = [sr, C2 * (dr - si), -di, -C2 * (dr + si)]
    e = [part_a[a] + part_b[a] for a in range(4)] + [part_a[a] - part_b[a] for a in range(4)]
    (r1, i1), (r3, i3), (r5, i5), (r7, i7) = h[1], h[3], h[5], h[7]
    p17, m17, p35, m35 = r1 + r7, r1 - r7, r3 + r5, r3 - r5
    sums = [p17 + p35, C1 * m17 + C3 * m35, C2 * (p17 - p35), C3 * m17 - C1 * m35]
    ip17, im17, ip35, im35 = i1 + i7, i1 - i7, i3 + i5, i3 - i5
    q1 = C3 * ip17 + C1 * ip35
    q2 = C2 * (im17 + im35)
    q3 = C1 * ip17 - C3 * ip35
    q4 = im17 - im35
    o = [
        sums[0],
        sums[1] - q1,
        sums[2] - q2,
        sums[3] - q3,
        -q4,
        -sums[3] - q3,
        -sums[2] - q2,
        -sums[1] - q1,
    ]
    return [e[a] + o[a] for a in range(8)] + [e[a] - o[a] for a in range(8)]


def forward_kernel(f, fwd, ss, s2, edges, resp, nyq, wave, out_edge, xh, xm, xl, ends_all):
    step = 16

    def radix(t, carry):
        rows = pl.ds(pl.multiple_of(t * step, step), step)
        far_rows = pl.ds(pl.multiple_of(128 + t * step, step), step)
        parts = radix_forward([f[a, rows, :] for a in range(16)])
        for slot in range(SLOTS):
            for where, value in ((rows, parts[slot][0]), (far_rows, parts[slot][1])):
                xh[slot, where, :], xm[slot, where, :], xl[slot, where, :] = split3(value)
        return carry

    lax.fori_loop(0, 128 // step, radix, 0, unroll=RADIX_UNROLL)

    def to_frequency(s):
        wide = dot(fwd[s], jnp.concatenate([xh[s], xm[s]], axis=1))
        spec = dot(fwd[s, 0:256], xl[s]) + wide[512:768, 0:128]
        spec += wide[256:512, 0:128] + wide[0:256, 128:256] + wide[256:512, 128:256]
        return spec + wide[0:256, 0:128]

    def to_sine(s, spec):
        high, mid, low = split3(spec)
        wide = dot(jnp.concatenate([high, mid], axis=1), ss[...])
        bent = dot(jnp.concatenate([high, low], axis=1), s2[...])
        bent += wide[:, 128:256] + wide[:, 0:128]
        wave[s] = bent
        return bent

    def to_ends(s, bent):
        high, mid = split2(bent * resp[s])
        ends = lax.dot_general(
            edges[...],
            jnp.concatenate([high, mid], axis=1),
            (((1,), (1,)), ((), ())),
            preferred_element_type=F32,
        )
        ends = ends[0:8] + ends[8:16]
        ends_all[0, s : s + 1] = ends[0:1]
        ends_all[1, s : s + 1] = ends[1:2]
        ends_all[2, s : s + 1] = ends[2:3] + (ends[0:1] - ends[1:2]) * nyq[s]

    for first in range(0, SLOTS, FGROUP):
        group = range(first, first + FGROUP)
        specs = [to_frequency(s) for s in group]
        waves = [to_sine(s, spec) for s, spec in zip(group, specs)]
        for s, bent in zip(group, waves):
            to_ends(s, bent)
    for e in range(GX):
        out_edge[e] = ends_all[...]


def backward_kernel(me, wave, ends, link, resp, ranks, back1, back2, inv, ind_out, grad_out, hs, invs, sems, parts_all, out_sems):
    copies = []
    for s in range(SLOTS):
        copy = pltpu.make_async_copy(inv.at[s], invs.at[s], sems.at[s])
        copy.start()
        copies.append(copy)
    left = jnp.zeros((SLOTS, 256), F32)
    right = jnp.zeros((SLOTS, 256), F32)
    swing = jnp.zeros((SLOTS, 256), F32)
    for e in range(GX):
        n = (me[0] - e + GX) % GX
        first, last = ends[e, 0], ends[e, 1]
        near = link[0, n]
        left += near * first + link[1, (GX - n) % GX] * last
        right += link[1, n] * first + near * last
        swing += ends[e, 2]
    swing *= 1.0 / NX
    values = []
    for value in (left, right, swing):
        high = value.astype(BF16).astype(F32)
        values.append((high, value - high))

    def couple(s):
        highs = [high[s : s + 1] for high, _ in values]
        mids = [mid[s : s + 1] for _, mid in values]
        stack = jnp.concatenate(highs + mids + highs + [jnp.zeros((7, 256), F32)], axis=0)
        return lax.dot_general(
            stack.astype(BF16), ranks[...], (((0,), (0,)), ((), ())), preferred_element_type=F32
        )

    def to_columns(s, wide):
        bent = resp[s] * (wave[s] - wide[:, 0:128]) - wide[:, 128:256]
        high, mid = split2(bent)
        line = dot(jnp.concatenate([high, mid], axis=1), back1[...]) + dot(high, back2[...])
        return jnp.concatenate([line[:, 0:128], line[:, 128:256] + wide[:, 256:384]], axis=1)

    def to_rows(s, line):
        high, mid = split2(line)
        copies[s].wait()
        wide = dot(invs[s], high)
        hs[s] = dot(invs[s, 0:256], mid) + wide[256:512] + wide[0:256]

    for first in range(0, SLOTS, BGROUP):
        group = range(first, first + BGROUP)
        wides = [couple(s) for s in group]
        lines = [to_columns(s, wide) for s, wide in zip(group, wides)]
        for s, line in zip(group, lines):
            to_rows(s, line)
    step = 8
    chunk = 128 // CHUNKS
    outgoing = []

    def send(part, rows):
        target = (ind_out, grad_out.at[0], grad_out.at[1])[part]
        copy = pltpu.make_async_copy(
            parts_all.at[part, :, rows, :], target.at[:, rows, :], out_sems.at[len(outgoing)]
        )
        copy.start()
        outgoing.append(copy)

    ind, grad_x, grad_y = parts_all.at[0], parts_all.at[1], parts_all.at[2]
    for c in reversed(range(CHUNKS)):

        def radix(t, carry):
            start = c * chunk + t * step
            rows = pl.ds(pl.multiple_of(start, step), step)
            far_rows = pl.ds(pl.multiple_of(128 + start, step), step)
            for part in range(2):
                lanes = slice(128 * part, 128 * part + 128)
                values = radix_inverse(
                    [(hs[s, rows, lanes], hs[s, far_rows, lanes]) for s in range(SLOTS)]
                )
                for a in range(16):
                    parts_all[part, a, rows, :] = values[a]
            return carry

        lax.fori_loop(0, chunk // step, radix, 0, unroll=RADIX_UNROLL)
        rows = pl.ds(c * chunk, chunk)
        send(0, rows)
        send(1, rows)
        low, high = c * chunk, min((c + 1) * chunk, 127)
        for a in range(16):
            grad_y[a, low:high, :] = ind[a, low + 1 : high + 1, :] - ind[a, low:high, :]
        if c < CHUNKS - 1:
            send(2, rows)
    for a in range(16):
        grad_y[a, 127:128, :] = ind[(a + 1) % 16, 0:1, :] - ind[a, 127:128, :]
    send(2, pl.ds(128 - chunk, chunk))
    for copy in outgoing:
        copy.wait()


def vmem():
    return pl.BlockSpec(memory_space=pltpu.VMEM)


def smem():
    return pl.BlockSpec(memory_space=pltpu.SMEM)


def params(mib):
    return pltpu.CompilerParams(vmem_limit_bytes=mib * 1024 * 1024)


def pack(owner, brick, fill, normals, fractions, offsets):
    return pl.pallas_call(
        pack_kernel,
        out_shape=jax.ShapeDtypeStruct((DEV, 5, 4, 128), F32),
        in_specs=[smem()] * 3 + [vmem()] * 3,
        out_specs=vmem(),
        scratch_shapes=[pltpu.SMEM((DEV,), jnp.int32)],
        compiler_params=params(56),
        interpret=INTERPRET,
        name="pack",
    )(owner, brick, fill, normals, fractions, offsets)


def splat(recv):
    return pl.pallas_call(
        splat_kernel,
        out_shape=jax.ShapeDtypeStruct((Z, NY // GY, 128), F32),
        in_specs=[vmem()],
        out_specs=vmem(),
        scratch_shapes=[pltpu.VMEM((32, 96, 256), F32)],
        compiler_params=params(12),
        interpret=INTERPRET,
        name="splat",
    )(recv)


def hbm():
    return pl.BlockSpec(memory_space=pltpu.HBM)


def forward(f):
    t = tables()
    return pl.pallas_call(
        forward_kernel,
        out_shape=(
            jax.ShapeDtypeStruct((SLOTS, 256, 128), F32),
            jax.ShapeDtypeStruct((GX, 3, SLOTS, 256), F32),
        ),
        in_specs=[vmem()] * 7,
        out_specs=(vmem(), vmem()),
        scratch_shapes=[pltpu.VMEM((SLOTS, 256, 128), BF16)] * 3
        + [pltpu.VMEM((3, SLOTS, 256), F32)],
        compiler_params=params(LF),
        interpret=INTERPRET,
        name="forward",
    )(f, t["fwd"], t["ss"], t["s2"], t["edges"], t["resp"], t["nyq"])


def backward(me, wave, ends):
    t = tables()
    return pl.pallas_call(
        backward_kernel,
        out_shape=(
            jax.ShapeDtypeStruct((16, 128, 128), F32),
            jax.ShapeDtypeStruct((2, 16, 128, 128), F32),
        ),
        in_specs=[smem()] + [vmem()] * 7 + [hbm()],
        out_specs=(hbm(), hbm()),
        scratch_shapes=[
            pltpu.VMEM((SLOTS, 256, 256), F32),
            pltpu.VMEM((SLOTS, 512, 256), BF16),
            pltpu.SemaphoreType.DMA((SLOTS,)),
            pltpu.VMEM((3, 16, 128, 128), F32),
            pltpu.SemaphoreType.DMA((3 * CHUNKS,)),
        ],
        compiler_params=params(LB),
        interpret=INTERPRET,
        name="backward",
    )(me, wave, ends, t["link"], t["resp"], t["ranks"], t["back1"], t["back2"], t["inv"])


def shards(normals, fractions, offsets, owner, brick, fill):
    send = pack(owner[:, 0], brick, fill, normals, fractions, offsets)
    recv = lax.all_to_all(send, ("gx", "gy"), split_axis=0, concat_axis=0, tiled=True)
    tile = splat(recv)
    plane = lax.all_to_all(tile, "gy", split_axis=0, concat_axis=0, tiled=True)
    wave, edge = forward(plane.reshape(16, 128, 128))
    ends = lax.all_to_all(edge, "gx", split_axis=0, concat_axis=0, tiled=True)
    me = lax.axis_index("gx").astype(jnp.int32).reshape(1)
    ind, grad = backward(me, wave, ends)
    return ind.reshape(1, NY, 128), grad.reshape(2, 1, NY, 128)


def solution(mesh):
    in_specs = (
        P(("gx", "gy"), None, None),
        P(("gx", "gy"), None, None),
        P(("gx", "gy"), None),
        P(("gx", "gy"), None),
        P(("gx", "gy")),
        P(("gx", "gy")),
    )
    out_specs = (P("gy", None, "gx"), P(None, "gy", None, "gx"))
    return jax.shard_map(shards, mesh=mesh, in_specs=in_specs, out_specs=out_specs, check_vma=False)
```

```python
import functools
import math

import jax
import jax.numpy as jnp
import numpy as np
from jax import lax
from jax.experimental import pallas as pl
from jax.experimental.pallas import tpu as pltpu
from jax.sharding import PartitionSpec as P

NX = 2048
NY = 2048
Z = 8
BX = 128
BY = 8
P_SIZE = 256
GX = 16
GY = 8
DEV = GX * GY
ALPHA = 4e-06
SLOTS = 8
F32 = jnp.float32
BF16 = jnp.bfloat16
C1 = math.cos(math.pi / 8)
C2 = math.cos(math.pi / 4)
C3 = math.cos(3 * math.pi / 8)
INTERPRET = False
SPLAT_UNROLL = 32
FINISH_UNROLL = 16
FGROUP = 8
BGROUP = 4
RADIX_UNROLL = 2
CHUNKS = 4
LF = 24
LB = 51
LP = 56
PACK_UNROLL = 16


def np_split(values, parts):
    pieces = []
    rest = np.asarray(values, np.float64)
    for _ in range(parts):
        piece = rest.astype(BF16)
        pieces.append(piece)
        rest = rest - piece.astype(np.float64)
    return pieces


def slot_rows():
    ky = np.zeros((SLOTS, 256), np.int64)
    k2 = np.arange(128)
    half = np.arange(64)
    ky[0] = np.concatenate([16 * half, 16 * half, 8 + 16 * half, 8 + 16 * half])
    for slot in range(1, SLOTS):
        ky[slot] = np.concatenate([slot + 16 * k2, slot + 16 * k2])
    return ky


@functools.lru_cache(None)
def tables():
    ky = slot_rows()
    b = np.arange(128)
    fwd = np.zeros((SLOTS, 256, 256))
    weight = np.full((SLOTS, 256), 2.0 / NY)
    half = np.arange(64)
    for part in range(2):
        freq = part * 8 + 16 * half
        theta = 2 * np.pi * ((freq[:, None] * b[None, :]) % NY) / NY
        fwd[0, part * 128 : part * 128 + 64, part * 128 : part * 128 + 128] = np.cos(theta)
        fwd[0, part * 128 + 64 : part * 128 + 128, part * 128 : part * 128 + 128] = -np.sin(theta)
    weight[0, 0] = 1.0 / NY
    for slot in range(1, SLOTS):
        freq = slot + 16 * np.arange(128)
        theta = 2 * np.pi * ((freq[:, None] * b[None, :]) % NY) / NY
        cos, sin = np.cos(theta), np.sin(theta)
        fwd[slot] = np.block([[cos, sin], [-sin, cos]])
    inv = np.transpose(fwd, (0, 2, 1)) * weight[:, None, :]
    c = 4 * np.sin(np.pi * np.minimum(ky, NY - ky) / NY) ** 2 + ALPHA
    j = np.arange(1, 129)
    mu = 4 * np.sin(np.pi * j / 258) ** 2
    resp = -1.0 / (mu[None, None, :] + c[:, :, None])
    x = np.arange(128)
    sine = np.sqrt(2 / 129) * np.sin(np.pi * (x[:, None] + 1) * j[None, :] / 129)
    alt = ((-1.0) ** x) @ sine
    edge = np.zeros((8, 128))
    edge[0], edge[1], edge[2] = sine[0], sine[127], alt
    nyq = 1.0 / (-4.0 - c)
    root = np.sqrt(c * (c + 4))
    big = 1 + c / 2 + root / 2
    logr = -np.log(big)

    def green(n):
        n = n % NX
        return -(np.exp(logr * n) + np.exp(logr * (NX - n))) / (root * (1 - np.exp(logr * NX)))

    link = np.zeros((2, GX, SLOTS, 256))
    for n in range(GX):
        link[0, n] = -green(128 * n)
        link[1, n] = -green(128 * (n + 1) + 1) + (1.0 if n == GX - 1 else 0.0)
    fh, fm, fl = np_split(fwd, 3)
    ih, im = np_split(inv, 2)
    sh, sm, sl = np_split(sine, 3)
    ss = np.block([[sh, sm], [sh, sm]])
    s2 = np.concatenate([sl, sh], axis=0)
    eh, em = np_split(edge, 2)
    edges = np.block([[eh, eh], [em, em]])
    back = np.concatenate([sine.T, np.concatenate([sine.T[:, 1:], np.zeros((128, 1))], axis=1) - sine.T], axis=1)
    bh, bm = np_split(back, 2)
    back1 = np.concatenate([bh, bh], axis=0)
    rank = np.zeros((3, 384))
    rank[0, 0:128] = sine[0]
    rank[1, 0:128] = sine[127]
    rank[2, 128:256] = alt
    rank[1, 256 + 127] = 1.0
    rank[2, 256 + 127] = -1.0
    rh, rm = np_split(rank, 2)
    ranks = np.concatenate([rh, rh, rm, np.zeros((7, 384), BF16)], axis=0)
    f = np.float32
    return dict(
        fwd=np.concatenate([fh, fm, fl], axis=1), inv=np.concatenate([ih, im], axis=1), ss=ss, s2=s2,
        edges=edges, resp=resp.astype(f), nyq=nyq.reshape(SLOTS, 1, 256).astype(f),
        link=link.astype(f), back1=back1, back2=bm, ranks=ranks,
    )


def split2(value):
    high = value.astype(BF16)
    return high, (value - high.astype(F32)).astype(BF16)


def split3(value):
    high = value.astype(BF16)
    rest = value - high.astype(F32)
    mid = rest.astype(BF16)
    return high, mid, (rest - mid.astype(F32)).astype(BF16)


def dot(left, right):
    return jnp.dot(left, right, preferred_element_type=F32)


def pack_kernel(owner, brick, fill, normals, fractions, offsets, send, counts):
    blocks = normals.shape[0]

    def clear(d, carry):
        counts[d] = 0
        send[d, 4] = jnp.full((4, 128), -1.0, F32)
        return carry

    lax.fori_loop(0, DEV, clear, 0, unroll=8)
    lane = lax.broadcasted_iota(jnp.int32, (2, 256), 1)
    row4 = lax.broadcasted_iota(jnp.int32, (4, 128), 0)

    def one(b, carry):
        d = owner[b]
        slot = counts[d]
        counts[d] = slot + 1
        live = jnp.where(lane < fill[b], normals[b], 0.0)
        frac = fractions[b]
        send[d, 2 * slot] = jnp.concatenate([live[:, :128], live[:, 128:]], axis=0)
        send[d, 2 * slot + 1] = jnp.concatenate(
            [frac[1:2, :128], frac[0:1, :128], frac[1:2, 128:], frac[0:1, 128:]], axis=0
        )
        cell = (offsets[pl.ds(b, 1), :] + brick[b] * (Z * BY * BX)).astype(F32)
        two = jnp.concatenate([cell[:, :128], cell[:, 128:]], axis=0)
        send[d, 4] = jnp.where(row4 // 2 == slot, jnp.concatenate([two, two], axis=0), send[d, 4])
        return carry

    lax.fori_loop(0, blocks, one, 0, unroll=PACK_UNROLL)


def splat_kernel(recv, out, acc):
    bricks = acc.shape[0]

    def clear(l, carry):
        acc[l] = jnp.zeros(acc.shape[1:], F32)
        return carry

    lax.fori_loop(0, bricks, clear, 0)
    rows = lax.broadcasted_iota(jnp.int32, (32, 128), 0).astype(F32).astype(BF16)
    cols = lax.broadcasted_iota(jnp.int32, (256, 128), 0).astype(F32).astype(BF16)
    zero = jnp.zeros((), BF16)
    one_b = jnp.ones((), BF16)

    def spread(row, count):
        tile = jnp.broadcast_to(row, (16, 128)).astype(BF16)
        return jnp.concatenate([tile] * (count // 16), axis=0)

    def build(d, slot):
        cell2 = recv[d, 4][2 * slot : 2 * slot + 2].astype(jnp.int32)
        filled = cell2[0:1] >= 0
        norm = jnp.where(filled, recv[d, 2 * slot], 0.0)
        frac = jnp.where(filled, recv[d, 2 * slot + 1], 0.0)
        far = norm * frac
        near = norm * (1.0 - frac)
        near_h = near.astype(BF16).astype(F32)
        far_h = far.astype(BF16).astype(F32)
        near_l = near - near_h
        far_l = far - far_h
        line2 = (((cell2 >> 11) & 3) * 8 + ((cell2 >> 7) & 7)).astype(F32)
        next2 = line2 + 1.0
        col2 = (((cell2 >> 10) & 1) * 128 + (cell2 & 127)).astype(F32)
        left, right = [], []
        for half in range(2):
            here = spread(line2[half : half + 1], 32) == rows
            below = spread(next2[half : half + 1], 32) == rows
            x = 2 * half
            parts = []
            for near_v, far_v in ((near_h, far_h), (near_l, far_l)):
                parts.append(
                    jnp.where(
                        here,
                        spread(near_v[x : x + 1], 32),
                        jnp.where(below, spread(far_v[x : x + 1], 32), zero),
                    )
                )
                parts.append(jnp.where(here, spread(near_v[x + 1 : x + 2], 32), zero))
                parts.append(jnp.where(here, spread(far_v[x + 1 : x + 2], 32), zero))
            left.append(jnp.concatenate(parts, axis=0))
            right.append(jnp.where(spread(col2[half : half + 1], 256) == cols, one_b, zero))
        piece = lax.dot_general(
            jnp.concatenate(left, axis=1),
            jnp.concatenate(right, axis=1),
            (((1,), (1,)), ((), ())),
            preferred_element_type=F32,
        )
        return piece[0:96] + piece[96:192], jnp.maximum(cell2[0, 0] >> 13, 0)

    group = 2 * SPLAT_UNROLL

    def one(i, carry):
        for piece, l in [build(i * SPLAT_UNROLL + k // 2, k % 2) for k in range(group)]:
            acc[l] += piece
        return carry

    lax.fori_loop(0, DEV // SPLAT_UNROLL, one, 0)

    def finish(l, carry):
        for odd in range(2):
            lanes = slice(128 * odd, 128 * odd + 128)
            flux_x = acc[l, 0:32, lanes]
            near_y = acc[l, 32:64, lanes].reshape(4, BY, 128)
            far_y = acc[l, 64:96, lanes].reshape(4, BY, 128)
            near_y = near_y - pltpu.roll(near_y, 1, axis=1)
            far_y = far_y - pltpu.roll(far_y, 1, axis=1)
            moved = pltpu.roll(far_y.reshape(32, 128) - flux_x, 1, axis=1)
            tile = (flux_x + near_y.reshape(32, 128) + moved).reshape(4, BY, 128)
            for plane in range(4):
                out[2 * plane + odd, pl.ds(pl.multiple_of(l * BY, BY), BY), :] = tile[plane]
        return carry

    lax.fori_loop(0, bricks, finish, 0, unroll=FINISH_UNROLL)


def radix_forward(f):
    e = [f[a] + f[a + 8] for a in range(8)]
    o = [f[a] - f[a + 8] for a in range(8)]
    p = [e[a] + e[a + 4] for a in range(4)]
    q = [e[a] - e[a + 4] for a in range(4)]
    even, odd = p[0] + p[2], p[1] + p[3]
    out = [None] * 8
    out[0] = (even + odd, even - odd)
    out[4] = (p[0] - p[2], p[3] - p[1])
    t1 = C2 * (q[1] - q[3])
    t2 = C2 * (q[1] + q[3])
    out[2] = (q[0] + t1, -(q[2] + t2))
    out[6] = (q[0] - t1, q[2] - t2)
    d = [None] + [o[a] - o[8 - a] for a in range(1, 4)]
    s = [None] + [o[a] + o[8 - a] for a in range(1, 4)]
    d2, s2 = C2 * d[2], C2 * s[2]
    base_p, base_m = o[0] + d2, o[0] - d2
    u1 = C1 * d[1] + C3 * d[3]
    u3 = C3 * d[1] - C1 * d[3]
    v1 = C3 * s[1] + C1 * s[3]
    v3 = C1 * s[1] - C3 * s[3]
    w_p, w_m = s2 + o[4], s2 - o[4]
    out[1] = (base_p + u1, -(v1 + w_p))
    out[7] = (base_p - u1, w_p - v1)
    out[3] = (base_m + u3, -(v3 + w_m))
    out[5] = (base_m - u3, w_m - v3)
    return out


def radix_inverse(h):
    (h0, h8) = h[0]
    plus, minus = h0 + h8, h0 - h8
    r4, i4 = h[4]
    part_a = [plus + r4, minus - i4, plus - r4, minus + i4]
    (r2, i2), (r6, i6) = h[2], h[6]
    dr, sr = r2 - r6, r2 + r6
    di, si = i2 - i6, i2 + i6
    part_b = [sr, C2 * (dr - si), -di, -C2 * (dr + si)]
    e = [part_a[a] + part_b[a] for a in range(4)] + [part_a[a] - part_b[a] for a in range(4)]
    (r1, i1), (r3, i3), (r5, i5), (r7, i7) = h[1], h[3], h[5], h[7]
    p17, m17, p35, m35 = r1 + r7, r1 - r7, r3 + r5, r3 - r5
    sums = [p17 + p35, C1 * m17 + C3 * m35, C2 * (p17 - p35), C3 * m17 - C1 * m35]
    ip17, im17, ip35, im35 = i1 + i7, i1 - i7, i3 + i5, i3 - i5
    q1 = C3 * ip17 + C1 * ip35
    q2 = C2 * (im17 + im35)
    q3 = C1 * ip17 - C3 * ip35
    q4 = im17 - im35
    o = [
        sums[0],
        sums[1] - q1,
        sums[2] - q2,
        sums[3] - q3,
        -q4,
        -sums[3] - q3,
        -sums[2] - q2,
        -sums[1] - q1,
    ]
    return [e[a] + o[a] for a in range(8)] + [e[a] - o[a] for a in range(8)]


def forward_kernel(f, fwd, ss, s2, edges, resp, nyq, wave, out_edge, xh, xm, xl, ends_all):
    step = 16

    def radix(t, carry):
        rows = pl.ds(pl.multiple_of(t * step, step), step)
        far_rows = pl.ds(pl.multiple_of(128 + t * step, step), step)
        parts = radix_forward([f[a, rows, :] for a in range(16)])
        for slot in range(SLOTS):
            for where, value in ((rows, parts[slot][0]), (far_rows, parts[slot][1])):
                xh[slot, where, :], xm[slot, where, :], xl[slot, where, :] = split3(value)
        return carry

    lax.fori_loop(0, 128 // step, radix, 0, unroll=RADIX_UNROLL)

    def to_frequency(s):
        wide = dot(fwd[s], jnp.concatenate([xh[s], xm[s]], axis=1))
        spec = dot(fwd[s, 0:256], xl[s]) + wide[512:768, 0:128]
        spec += wide[256:512, 0:128] + wide[0:256, 128:256] + wide[256:512, 128:256]
        return spec + wide[0:256, 0:128]

    def to_sine(s, spec):
        high, mid, low = split3(spec)
        wide = dot(jnp.concatenate([high, mid], axis=1), ss[...])
        bent = dot(jnp.concatenate([high, low], axis=1), s2[...])
        bent += wide[:, 128:256] + wide[:, 0:128]
        wave[s] = bent
        return bent

    def to_ends(s, bent):
        high, mid = split2(bent * resp[s])
        ends = lax.dot_general(
            edges[...],
            jnp.concatenate([high, mid], axis=1),
            (((1,), (1,)), ((), ())),
            preferred_element_type=F32,
        )
        ends = ends[0:8] + ends[8:16]
        ends_all[0, s : s + 1] = ends[0:1]
        ends_all[1, s : s + 1] = ends[1:2]
        ends_all[2, s : s + 1] = ends[2:3] + (ends[0:1] - ends[1:2]) * nyq[s]

    for first in range(0, SLOTS, FGROUP):
        group = range(first, first + FGROUP)
        specs = [to_frequency(s) for s in group]
        waves = [to_sine(s, spec) for s, spec in zip(group, specs)]
        for s, bent in zip(group, waves):
            to_ends(s, bent)
    for e in range(GX):
        out_edge[e] = ends_all[...]


def backward_kernel(me, wave, ends, link, resp, ranks, back1, back2, inv, ind_out, grad_out, hs, invs, sems, parts_all, out_sems):
    copies = []
    for s in range(SLOTS):
        copy = pltpu.make_async_copy(inv.at[s], invs.at[s], sems.at[s])
        copy.start()
        copies.append(copy)
    left = jnp.zeros((SLOTS, 256), F32)
    right = jnp.zeros((SLOTS, 256), F32)
    swing = jnp.zeros((SLOTS, 256), F32)
    for e in range(GX):
        n = (me[0] - e + GX) % GX
        first, last = ends[e, 0], ends[e, 1]
        near = link[0, n]
        left += near * first + link[1, (GX - n) % GX] * last
        right += link[1, n] * first + near * last
        swing += ends[e, 2]
    swing *= 1.0 / NX
    values = []
    for value in (left, right, swing):
        high = value.astype(BF16).astype(F32)
        values.append((high, value - high))

    def couple(s):
        highs = [high[s : s + 1] for high, _ in values]
        mids = [mid[s : s + 1] for _, mid in values]
        stack = jnp.concatenate(highs + mids + highs + [jnp.zeros((7, 256), F32)], axis=0)
        return lax.dot_general(
            stack.astype(BF16), ranks[...], (((0,), (0,)), ((), ())), preferred_element_type=F32
        )

    def to_columns(s, wide):
        bent = resp[s] * (wave[s] - wide[:, 0:128]) - wide[:, 128:256]
        high, mid = split2(bent)
        line = dot(jnp.concatenate([high, mid], axis=1), back1[...]) + dot(high, back2[...])
        return jnp.concatenate([line[:, 0:128], line[:, 128:256] + wide[:, 256:384]], axis=1)

    def to_rows(s, line):
        high, mid = split2(line)
        copies[s].wait()
        wide = dot(invs[s], high)
        hs[s] = dot(invs[s, 0:256], mid) + wide[256:512] + wide[0:256]

    for first in range(0, SLOTS, BGROUP):
        group = range(first, first + BGROUP)
        wides = [couple(s) for s in group]
        lines = [to_columns(s, wide) for s, wide in zip(group, wides)]
        for s, line in zip(group, lines):
            to_rows(s, line)
    step = 8
    chunk = 128 // CHUNKS
    outgoing = []

    def send(part, rows):
        target = (ind_out, grad_out.at[0], grad_out.at[1])[part]
        copy = pltpu.make_async_copy(
            parts_all.at[part, :, rows, :], target.at[:, rows, :], out_sems.at[len(outgoing)]
        )
        copy.start()
        outgoing.append(copy)

    ind, grad_x, grad_y = parts_all.at[0], parts_all.at[1], parts_all.at[2]
    for c in reversed(range(CHUNKS)):

        def radix(t, carry):
            start = c * chunk + t * step
            rows = pl.ds(pl.multiple_of(start, step), step)
            far_rows = pl.ds(pl.multiple_of(128 + start, step), step)
            for part in range(2):
                lanes = slice(128 * part, 128 * part + 128)
                values = radix_inverse(
                    [(hs[s, rows, lanes], hs[s, far_rows, lanes]) for s in range(SLOTS)]
                )
                for a in range(16):
                    parts_all[part, a, rows, :] = values[a]
            return carry

        lax.fori_loop(0, chunk // step, radix, 0, unroll=RADIX_UNROLL)
        rows = pl.ds(c * chunk, chunk)
        send(0, rows)
        send(1, rows)
        low, high = c * chunk, min((c + 1) * chunk, 127)
        for a in range(16):
            grad_y[a, low:high, :] = ind[a, low + 1 : high + 1, :] - ind[a, low:high, :]
        if c < CHUNKS - 1:
            send(2, rows)
    for a in range(16):
        grad_y[a, 127:128, :] = ind[(a + 1) % 16, 0:1, :] - ind[a, 127:128, :]
    send(2, pl.ds(128 - chunk, chunk))
    for copy in outgoing:
        copy.wait()


def vmem():
    return pl.BlockSpec(memory_space=pltpu.VMEM)


def smem():
    return pl.BlockSpec(memory_space=pltpu.SMEM)


def params(mib):
    return pltpu.CompilerParams(vmem_limit_bytes=int(mib * 1024 * 1024))


def pack(owner, brick, fill, normals, fractions, offsets):
    return pl.pallas_call(
        pack_kernel,
        out_shape=jax.ShapeDtypeStruct((DEV, 5, 4, 128), F32),
        in_specs=[smem()] * 3 + [vmem()] * 3,
        out_specs=vmem(),
        scratch_shapes=[pltpu.SMEM((DEV,), jnp.int32)],
        compiler_params=params(LP),
        interpret=INTERPRET,
        name="pack",
    )(owner, brick, fill, normals, fractions, offsets)


def splat(recv):
    return pl.pallas_call(
        splat_kernel,
        out_shape=jax.ShapeDtypeStruct((Z, NY // GY, 128), F32),
        in_specs=[vmem()],
        out_specs=vmem(),
        scratch_shapes=[pltpu.VMEM((32, 96, 256), F32)],
        compiler_params=params(12),
        interpret=INTERPRET,
        name="splat",
    )(recv)


def hbm():
    return pl.BlockSpec(memory_space=pltpu.HBM)


def forward(f):
    t = tables()
    return pl.pallas_call(
        forward_kernel,
        out_shape=(
            jax.ShapeDtypeStruct((SLOTS, 256, 128), F32),
            jax.ShapeDtypeStruct((GX, 3, SLOTS, 256), F32),
        ),
        in_specs=[vmem()] * 7,
        out_specs=(vmem(), vmem()),
        scratch_shapes=[pltpu.VMEM((SLOTS, 256, 128), BF16)] * 3
        + [pltpu.VMEM((3, SLOTS, 256), F32)],
        compiler_params=params(LF),
        interpret=INTERPRET,
        name="forward",
    )(f, t["fwd"], t["ss"], t["s2"], t["edges"], t["resp"], t["nyq"])


def backward(me, wave, ends):
    t = tables()
    return pl.pallas_call(
        backward_kernel,
        out_shape=(
            jax.ShapeDtypeStruct((16, 128, 128), F32),
            jax.ShapeDtypeStruct((2, 16, 128, 128), F32),
        ),
        in_specs=[smem()] + [vmem()] * 7 + [hbm()],
        out_specs=(hbm(), hbm()),
        scratch_shapes=[
            pltpu.VMEM((SLOTS, 256, 256), F32),
            pltpu.VMEM((SLOTS, 512, 256), BF16),
            pltpu.SemaphoreType.DMA((SLOTS,)),
            pltpu.VMEM((3, 16, 128, 128), F32),
            pltpu.SemaphoreType.DMA((3 * CHUNKS,)),
        ],
        compiler_params=params(LB),
        interpret=INTERPRET,
        name="backward",
    )(me, wave, ends, t["link"], t["resp"], t["ranks"], t["back1"], t["back2"], t["inv"])


def shards(normals, fractions, offsets, owner, brick, fill):
    send = pack(owner[:, 0], brick, fill, normals, fractions, offsets)
    recv = lax.all_to_all(send, ("gx", "gy"), split_axis=0, concat_axis=0, tiled=True)
    tile = splat(recv)
    plane = lax.all_to_all(tile, "gy", split_axis=0, concat_axis=0, tiled=True)
    wave, edge = forward(plane.reshape(16, 128, 128))
    ends = lax.all_to_all(edge, "gx", split_axis=0, concat_axis=0, tiled=True)
    me = lax.axis_index("gx").astype(jnp.int32).reshape(1)
    ind, grad = backward(me, wave, ends)
    return ind.reshape(1, NY, 128), grad.reshape(2, 1, NY, 128)


def solution(mesh):
    in_specs = (
        P(("gx", "gy"), None, None),
        P(("gx", "gy"), None, None),
        P(("gx", "gy"), None),
        P(("gx", "gy"), None),
        P(("gx", "gy")),
        P(("gx", "gy")),
    )
    out_specs = (P("gy", None, "gx"), P(None, "gy", None, "gx"))
    return jax.shard_map(shards, mesh=mesh, in_specs=in_specs, out_specs=out_specs, check_vma=False)
```

```python
import functools
import math

import jax
import jax.numpy as jnp
import numpy as np
from jax import lax
from jax.experimental import pallas as pl
from jax.experimental.pallas import tpu as pltpu
from jax.sharding import PartitionSpec as P

NX = 2048
NY = 2048
Z = 8
BX = 128
BY = 8
P_SIZE = 256
GX = 16
GY = 8
DEV = GX * GY
ALPHA = 4e-06
SLOTS = 8
F32 = jnp.float32
BF16 = jnp.bfloat16
C1 = math.cos(math.pi / 8)
C2 = math.cos(math.pi / 4)
C3 = math.cos(3 * math.pi / 8)
INTERPRET = False
SPLAT_UNROLL = 32
FINISH_UNROLL = 16
FGROUP = 8
BGROUP = 4
RADIX_UNROLL = 2
CHUNKS = 4
LF = 24
LB = 51
LP = 56
PACK_UNROLL = 16


def np_split(values, parts):
    pieces = []
    rest = np.asarray(values, np.float64)
    for _ in range(parts):
        piece = rest.astype(BF16)
        pieces.append(piece)
        rest = rest - piece.astype(np.float64)
    return pieces


def slot_rows():
    ky = np.zeros((SLOTS, 256), np.int64)
    k2 = np.arange(128)
    half = np.arange(64)
    ky[0] = np.concatenate([16 * half, 16 * half, 8 + 16 * half, 8 + 16 * half])
    for slot in range(1, SLOTS):
        ky[slot] = np.concatenate([slot + 16 * k2, slot + 16 * k2])
    return ky


@functools.lru_cache(None)
def tables():
    ky = slot_rows()
    b = np.arange(128)
    fwd = np.zeros((SLOTS, 256, 256))
    weight = np.full((SLOTS, 256), 2.0 / NY)
    half = np.arange(64)
    for part in range(2):
        freq = part * 8 + 16 * half
        theta = 2 * np.pi * ((freq[:, None] * b[None, :]) % NY) / NY
        fwd[0, part * 128 : part * 128 + 64, part * 128 : part * 128 + 128] = np.cos(theta)
        fwd[0, part * 128 + 64 : part * 128 + 128, part * 128 : part * 128 + 128] = -np.sin(theta)
    weight[0, 0] = 1.0 / NY
    for slot in range(1, SLOTS):
        freq = slot + 16 * np.arange(128)
        theta = 2 * np.pi * ((freq[:, None] * b[None, :]) % NY) / NY
        cos, sin = np.cos(theta), np.sin(theta)
        fwd[slot] = np.block([[cos, sin], [-sin, cos]])
    inv = np.transpose(fwd, (0, 2, 1)) * weight[:, None, :]
    c = 4 * np.sin(np.pi * np.minimum(ky, NY - ky) / NY) ** 2 + ALPHA
    j = np.arange(1, 129)
    mu = 4 * np.sin(np.pi * j / 258) ** 2
    resp = -1.0 / (mu[None, None, :] + c[:, :, None])
    x = np.arange(128)
    sine = np.sqrt(2 / 129) * np.sin(np.pi * (x[:, None] + 1) * j[None, :] / 129)
    alt = ((-1.0) ** x) @ sine
    edge = np.zeros((8, 128))
    edge[0], edge[1], edge[2] = sine[0], sine[127], alt
    nyq = 1.0 / (-4.0 - c)
    root = np.sqrt(c * (c + 4))
    big = 1 + c / 2 + root / 2
    logr = -np.log(big)

    def green(n):
        n = n % NX
        return -(np.exp(logr * n) + np.exp(logr * (NX - n))) / (root * (1 - np.exp(logr * NX)))

    link = np.zeros((2, GX, SLOTS, 256))
    for n in range(GX):
        link[0, n] = -green(128 * n)
        link[1, n] = -green(128 * (n + 1) + 1) + (1.0 if n == GX - 1 else 0.0)
    fh, fm, fl = np_split(fwd, 3)
    ih, im = np_split(inv, 2)
    sh, sm, sl = np_split(sine, 3)
    ss = np.block([[sh, sm], [sh, sm]])
    s2 = np.concatenate([sl, sh], axis=0)
    eh, em = np_split(edge, 2)
    edges = np.block([[eh, eh], [em, em]])
    back = np.concatenate([sine.T, np.concatenate([sine.T[:, 1:], np.zeros((128, 1))], axis=1) - sine.T], axis=1)
    bh, bm = np_split(back, 2)
    back1 = np.concatenate([bh, bh], axis=0)
    rank = np.zeros((3, 384))
    rank[0, 0:128] = sine[0]
    rank[1, 0:128] = sine[127]
    rank[2, 128:256] = alt
    rank[1, 256 + 127] = 1.0
    rank[2, 256 + 127] = -1.0
    rh, rm = np_split(rank, 2)
    ranks = np.concatenate([rh, rh, rm, np.zeros((7, 384), BF16)], axis=0)
    f = np.float32
    return dict(
        fwd=np.concatenate([fh, fm, fl], axis=1), inv=np.concatenate([ih, im], axis=1), ss=ss, s2=s2,
        edges=edges, resp=resp.astype(f), nyq=nyq.reshape(SLOTS, 1, 256).astype(f),
        link=link.astype(f), back1=back1, back2=bm, ranks=ranks,
    )


def split2(value):
    high = value.astype(BF16)
    return high, (value - high.astype(F32)).astype(BF16)


def split3(value):
    high = value.astype(BF16)
    rest = value - high.astype(F32)
    mid = rest.astype(BF16)
    return high, mid, (rest - mid.astype(F32)).astype(BF16)


def dot(left, right):
    return jnp.dot(left, right, preferred_element_type=F32)


def pack_kernel(owner, brick, fill, normals, fractions, offsets, send, counts):
    blocks = normals.shape[0]

    def clear(d, carry):
        counts[d] = 0
        send[d, 4] = jnp.full((4, 128), -1.0, F32)
        return carry

    lax.fori_loop(0, DEV, clear, 0, unroll=8)
    lane = lax.broadcasted_iota(jnp.int32, (2, 256), 1)
    row4 = lax.broadcasted_iota(jnp.int32, (4, 128), 0)

    def one(b, carry):
        d = owner[b]
        slot = counts[d]
        counts[d] = slot + 1
        live = jnp.where(lane < fill[b], normals[b], 0.0)
        frac = fractions[b]
        send[d, 2 * slot] = jnp.concatenate([live[:, :128], live[:, 128:]], axis=0)
        send[d, 2 * slot + 1] = jnp.concatenate(
            [frac[1:2, :128], frac[0:1, :128], frac[1:2, 128:], frac[0:1, 128:]], axis=0
        )
        cell = (offsets[pl.ds(b, 1), :] + brick[b] * (Z * BY * BX)).astype(F32)
        two = jnp.concatenate([cell[:, :128], cell[:, 128:]], axis=0)
        send[d, 4] = jnp.where(row4 // 2 == slot, jnp.concatenate([two, two], axis=0), send[d, 4])
        return carry

    lax.fori_loop(0, blocks, one, 0, unroll=PACK_UNROLL)


def splat_kernel(recv, out, acc):
    bricks = acc.shape[0]

    def clear(l, carry):
        acc[l] = jnp.zeros(acc.shape[1:], F32)
        return carry

    lax.fori_loop(0, bricks, clear, 0)
    rows = lax.broadcasted_iota(jnp.int32, (32, 128), 0).astype(F32).astype(BF16)
    cols = lax.broadcasted_iota(jnp.int32, (256, 128), 0).astype(F32).astype(BF16)
    zero = jnp.zeros((), BF16)
    one_b = jnp.ones((), BF16)

    def spread(row, count):
        tile = jnp.broadcast_to(row, (16, 128)).astype(BF16)
        return jnp.concatenate([tile] * (count // 16), axis=0)

    def build(d, slot):
        cell2 = recv[d, 4][2 * slot : 2 * slot + 2].astype(jnp.int32)
        filled = cell2[0:1] >= 0
        norm = jnp.where(filled, recv[d, 2 * slot], 0.0)
        frac = jnp.where(filled, recv[d, 2 * slot + 1], 0.0)
        far = norm * frac
        near = norm * (1.0 - frac)
        near_h = near.astype(BF16).astype(F32)
        far_h = far.astype(BF16).astype(F32)
        near_l = near - near_h
        far_l = far - far_h
        line2 = (((cell2 >> 11) & 3) * 8 + ((cell2 >> 7) & 7)).astype(F32)
        next2 = line2 + 1.0
        col2 = (((cell2 >> 10) & 1) * 128 + (cell2 & 127)).astype(F32)
        left, right = [], []
        for half in range(2):
            here = spread(line2[half : half + 1], 32) == rows
            below = spread(next2[half : half + 1], 32) == rows
            x = 2 * half
            parts = []
            for near_v, far_v in ((near_h, far_h), (near_l, far_l)):
                parts.append(
                    jnp.where(
                        here,
                        spread(near_v[x : x + 1], 32),
                        jnp.where(below, spread(far_v[x : x + 1], 32), zero),
                    )
                )
                parts.append(jnp.where(here, spread(near_v[x + 1 : x + 2], 32), zero))
                parts.append(jnp.where(here, spread(far_v[x + 1 : x + 2], 32), zero))
            left.append(jnp.concatenate(parts, axis=0))
            right.append(jnp.where(spread(col2[half : half + 1], 256) == cols, one_b, zero))
        piece = lax.dot_general(
            jnp.concatenate(left, axis=1),
            jnp.concatenate(right, axis=1),
            (((1,), (1,)), ((), ())),
            preferred_element_type=F32,
        )
        return piece[0:96] + piece[96:192], jnp.maximum(cell2[0, 0] >> 13, 0)

    group = 2 * SPLAT_UNROLL

    def one(i, carry):
        for piece, l in [build(i * SPLAT_UNROLL + k // 2, k % 2) for k in range(group)]:
            acc[l] += piece
        return carry

    lax.fori_loop(0, DEV // SPLAT_UNROLL, one, 0)

    def finish(l, carry):
        for odd in range(2):
            lanes = slice(128 * odd, 128 * odd + 128)
            flux_x = acc[l, 0:32, lanes]
            near_y = acc[l, 32:64, lanes].reshape(4, BY, 128)
            far_y = acc[l, 64:96, lanes].reshape(4, BY, 128)
            near_y = near_y - pltpu.roll(near_y, 1, axis=1)
            far_y = far_y - pltpu.roll(far_y, 1, axis=1)
            moved = pltpu.roll(far_y.reshape(32, 128) - flux_x, 1, axis=1)
            tile = (flux_x + near_y.reshape(32, 128) + moved).reshape(4, BY, 128)
            for plane in range(4):
                out[2 * plane + odd, pl.ds(pl.multiple_of(l * BY, BY), BY), :] = tile[plane]
        return carry

    lax.fori_loop(0, bricks, finish, 0, unroll=FINISH_UNROLL)


def radix_forward(f):
    e = [f[a] + f[a + 8] for a in range(8)]
    o = [f[a] - f[a + 8] for a in range(8)]
    p = [e[a] + e[a + 4] for a in range(4)]
    q = [e[a] - e[a + 4] for a in range(4)]
    even, odd = p[0] + p[2], p[1] + p[3]
    out = [None] * 8
    out[0] = (even + odd, even - odd)
    out[4] = (p[0] - p[2], p[3] - p[1])
    t1 = C2 * (q[1] - q[3])
    t2 = C2 * (q[1] + q[3])
    out[2] = (q[0] + t1, -(q[2] + t2))
    out[6] = (q[0] - t1, q[2] - t2)
    d = [None] + [o[a] - o[8 - a] for a in range(1, 4)]
    s = [None] + [o[a] + o[8 - a] for a in range(1, 4)]
    d2, s2 = C2 * d[2], C2 * s[2]
    base_p, base_m = o[0] + d2, o[0] - d2
    u1 = C1 * d[1] + C3 * d[3]
    u3 = C3 * d[1] - C1 * d[3]
    v1 = C3 * s[1] + C1 * s[3]
    v3 = C1 * s[1] - C3 * s[3]
    w_p, w_m = s2 + o[4], s2 - o[4]
    out[1] = (base_p + u1, -(v1 + w_p))
    out[7] = (base_p - u1, w_p - v1)
    out[3] = (base_m + u3, -(v3 + w_m))
    out[5] = (base_m - u3, w_m - v3)
    return out


def radix_inverse(h):
    (h0, h8) = h[0]
    plus, minus = h0 + h8, h0 - h8
    r4, i4 = h[4]
    part_a = [plus + r4, minus - i4, plus - r4, minus + i4]
    (r2, i2), (r6, i6) = h[2], h[6]
    dr, sr = r2 - r6, r2 + r6
    di, si = i2 - i6, i2 + i6
    part_b = [sr, C2 * (dr - si), -di, -C2 * (dr + si)]
    e = [part_a[a] + part_b[a] for a in range(4)] + [part_a[a] - part_b[a] for a in range(4)]
    (r1, i1), (r3, i3), (r5, i5), (r7, i7) = h[1], h[3], h[5], h[7]
    p17, m17, p35, m35 = r1 + r7, r1 - r7, r3 + r5, r3 - r5
    sums = [p17 + p35, C1 * m17 + C3 * m35, C2 * (p17 - p35), C3 * m17 - C1 * m35]
    ip17, im17, ip35, im35 = i1 + i7, i1 - i7, i3 + i5, i3 - i5
    q1 = C3 * ip17 + C1 * ip35
    q2 = C2 * (im17 + im35)
    q3 = C1 * ip17 - C3 * ip35
    q4 = im17 - im35
    o = [
        sums[0],
        sums[1] - q1,
        sums[2] - q2,
        sums[3] - q3,
        -q4,
        -sums[3] - q3,
        -sums[2] - q2,
        -sums[1] - q1,
    ]
    return [e[a] + o[a] for a in range(8)] + [e[a] - o[a] for a in range(8)]


def forward_kernel(f, fwd, ss, s2, edges, resp, nyq, wave, out_edge, xh, xm, xl, ends_all):
    step = 16

    def radix(t, carry):
        rows = pl.ds(pl.multiple_of(t * step, step), step)
        far_rows = pl.ds(pl.multiple_of(128 + t * step, step), step)
        parts = radix_forward([f[a, rows, :] for a in range(16)])
        for slot in range(SLOTS):
            for where, value in ((rows, parts[slot][0]), (far_rows, parts[slot][1])):
                xh[slot, where, :], xm[slot, where, :], xl[slot, where, :] = split3(value)
        return carry

    lax.fori_loop(0, 128 // step, radix, 0, unroll=RADIX_UNROLL)

    def to_frequency(s):
        wide = dot(fwd[s], jnp.concatenate([xh[s], xm[s]], axis=1))
        spec = dot(fwd[s, 0:256], xl[s]) + wide[512:768, 0:128]
        spec += wide[256:512, 0:128] + wide[0:256, 128:256] + wide[256:512, 128:256]
        return spec + wide[0:256, 0:128]

    def to_sine(s, spec):
        high, mid, low = split3(spec)
        wide = dot(jnp.concatenate([high, mid], axis=1), ss[...])
        bent = dot(jnp.concatenate([high, low], axis=1), s2[...])
        bent += wide[:, 128:256] + wide[:, 0:128]
        wave[s] = bent
        return bent

    def to_ends(s, bent):
        high, mid = split2(bent * resp[s])
        ends = lax.dot_general(
            edges[...],
            jnp.concatenate([high, mid], axis=1),
            (((1,), (1,)), ((), ())),
            preferred_element_type=F32,
        )
        ends = ends[0:8] + ends[8:16]
        ends_all[0, s : s + 1] = ends[0:1]
        ends_all[1, s : s + 1] = ends[1:2]
        ends_all[2, s : s + 1] = ends[2:3] + (ends[0:1] - ends[1:2]) * nyq[s]

    for first in range(0, SLOTS, FGROUP):
        group = range(first, first + FGROUP)
        specs = [to_frequency(s) for s in group]
        waves = [to_sine(s, spec) for s, spec in zip(group, specs)]
        for s, bent in zip(group, waves):
            to_ends(s, bent)
    for e in range(GX):
        out_edge[e] = ends_all[...]


def backward_kernel(me, wave, ends, link, resp, ranks, back1, back2, inv, ind_out, grad_out, hs, invs, sems, parts_all, out_sems):
    copies = []
    for s in range(SLOTS):
        copy = pltpu.make_async_copy(inv.at[s], invs.at[s], sems.at[s])
        copy.start()
        copies.append(copy)
    left = jnp.zeros((SLOTS, 256), F32)
    right = jnp.zeros((SLOTS, 256), F32)
    swing = jnp.zeros((SLOTS, 256), F32)
    for e in range(GX):
        n = (me[0] - e + GX) % GX
        first, last = ends[e, 0], ends[e, 1]
        near = link[0, n]
        left += near * first + link[1, (GX - n) % GX] * last
        right += link[1, n] * first + near * last
        swing += ends[e, 2]
    swing *= 1.0 / NX
    values = []
    for value in (left, right, swing):
        high = value.astype(BF16).astype(F32)
        values.append((high, value - high))

    def couple(s):
        highs = [high[s : s + 1] for high, _ in values]
        mids = [mid[s : s + 1] for _, mid in values]
        stack = jnp.concatenate(highs + mids + highs + [jnp.zeros((7, 256), F32)], axis=0)
        return lax.dot_general(
            stack.astype(BF16), ranks[...], (((0,), (0,)), ((), ())), preferred_element_type=F32
        )

    def to_columns(s, wide):
        bent = resp[s] * (wave[s] - wide[:, 0:128]) - wide[:, 128:256]
        high, mid = split2(bent)
        line = dot(jnp.concatenate([high, mid], axis=1), back1[...]) + dot(high, back2[...])
        return jnp.concatenate([line[:, 0:128], line[:, 128:256] + wide[:, 256:384]], axis=1)

    def to_rows(s, line):
        high, mid = split2(line)
        copies[s].wait()
        wide = dot(invs[s], high)
        hs[s] = dot(invs[s, 0:256], mid) + wide[256:512] + wide[0:256]

    for first in range(0, SLOTS, BGROUP):
        group = range(first, first + BGROUP)
        wides = [couple(s) for s in group]
        lines = [to_columns(s, wide) for s, wide in zip(group, wides)]
        for s, line in zip(group, lines):
            to_rows(s, line)
    step = 8
    chunk = 128 // CHUNKS
    outgoing = []

    def send(part, rows):
        target = (ind_out, grad_out.at[0], grad_out.at[1])[part]
        copy = pltpu.make_async_copy(
            parts_all.at[part, :, rows, :], target.at[:, rows, :], out_sems.at[len(outgoing)]
        )
        copy.start()
        outgoing.append(copy)

    ind, grad_x, grad_y = parts_all.at[0], parts_all.at[1], parts_all.at[2]
    for c in reversed(range(CHUNKS)):

        rows_out = pl.ds(c * chunk, chunk)
        for part in range(2):
            lanes = slice(128 * part, 128 * part + 128)

            def radix(t, carry):
                start = c * chunk + t * step
                rows = pl.ds(pl.multiple_of(start, step), step)
                far_rows = pl.ds(pl.multiple_of(128 + start, step), step)
                values = radix_inverse(
                    [(hs[s, rows, lanes], hs[s, far_rows, lanes]) for s in range(SLOTS)]
                )
                for a in range(16):
                    parts_all[part, a, rows, :] = values[a]
                return carry

            lax.fori_loop(0, chunk // step, radix, 0, unroll=RADIX_UNROLL)
            send(part, rows_out)
        low, high = c * chunk, min((c + 1) * chunk, 127)
        for a in range(16):
            grad_y[a, low:high, :] = ind[a, low + 1 : high + 1, :] - ind[a, low:high, :]
        if c < CHUNKS - 1:
            send(2, rows_out)
    for a in range(16):
        grad_y[a, 127:128, :] = ind[(a + 1) % 16, 0:1, :] - ind[a, 127:128, :]
    send(2, pl.ds(128 - chunk, chunk))
    for copy in outgoing:
        copy.wait()


def vmem():
    return pl.BlockSpec(memory_space=pltpu.VMEM)


def smem():
    return pl.BlockSpec(memory_space=pltpu.SMEM)


def params(mib):
    return pltpu.CompilerParams(vmem_limit_bytes=int(mib * 1024 * 1024))


def pack(owner, brick, fill, normals, fractions, offsets):
    return pl.pallas_call(
        pack_kernel,
        out_shape=jax.ShapeDtypeStruct((DEV, 5, 4, 128), F32),
        in_specs=[smem()] * 3 + [vmem()] * 3,
        out_specs=vmem(),
        scratch_shapes=[pltpu.SMEM((DEV,), jnp.int32)],
        compiler_params=params(LP),
        interpret=INTERPRET,
        name="pack",
    )(owner, brick, fill, normals, fractions, offsets)


def splat(recv):
    return pl.pallas_call(
        splat_kernel,
        out_shape=jax.ShapeDtypeStruct((Z, NY // GY, 128), F32),
        in_specs=[vmem()],
        out_specs=vmem(),
        scratch_shapes=[pltpu.VMEM((32, 96, 256), F32)],
        compiler_params=params(12),
        interpret=INTERPRET,
        name="splat",
    )(recv)


def hbm():
    return pl.BlockSpec(memory_space=pltpu.HBM)


def forward(f):
    t = tables()
    return pl.pallas_call(
        forward_kernel,
        out_shape=(
            jax.ShapeDtypeStruct((SLOTS, 256, 128), F32),
            jax.ShapeDtypeStruct((GX, 3, SLOTS, 256), F32),
        ),
        in_specs=[vmem()] * 7,
        out_specs=(vmem(), vmem()),
        scratch_shapes=[pltpu.VMEM((SLOTS, 256, 128), BF16)] * 3
        + [pltpu.VMEM((3, SLOTS, 256), F32)],
        compiler_params=params(LF),
        interpret=INTERPRET,
        name="forward",
    )(f, t["fwd"], t["ss"], t["s2"], t["edges"], t["resp"], t["nyq"])


def backward(me, wave, ends):
    t = tables()
    return pl.pallas_call(
        backward_kernel,
        out_shape=(
            jax.ShapeDtypeStruct((16, 128, 128), F32),
            jax.ShapeDtypeStruct((2, 16, 128, 128), F32),
        ),
        in_specs=[smem()] + [vmem()] * 7 + [hbm()],
        out_specs=(hbm(), hbm()),
        scratch_shapes=[
            pltpu.VMEM((SLOTS, 256, 256), F32),
            pltpu.VMEM((SLOTS, 512, 256), BF16),
            pltpu.SemaphoreType.DMA((SLOTS,)),
            pltpu.VMEM((3, 16, 128, 128), F32),
            pltpu.SemaphoreType.DMA((3 * CHUNKS,)),
        ],
        compiler_params=params(LB),
        interpret=INTERPRET,
        name="backward",
    )(me, wave, ends, t["link"], t["resp"], t["ranks"], t["back1"], t["back2"], t["inv"])


def shards(normals, fractions, offsets, owner, brick, fill):
    send = pack(owner[:, 0], brick, fill, normals, fractions, offsets)
    recv = lax.all_to_all(send, ("gx", "gy"), split_axis=0, concat_axis=0, tiled=True)
    tile = splat(recv)
    plane = lax.all_to_all(tile, "gy", split_axis=0, concat_axis=0, tiled=True)
    wave, edge = forward(plane.reshape(16, 128, 128))
    ends = lax.all_to_all(edge, "gx", split_axis=0, concat_axis=0, tiled=True)
    me = lax.axis_index("gx").astype(jnp.int32).reshape(1)
    ind, grad = backward(me, wave, ends)
    return ind.reshape(1, NY, 128), grad.reshape(2, 1, NY, 128)


def solution(mesh):
    in_specs = (
        P(("gx", "gy"), None, None),
        P(("gx", "gy"), None, None),
        P(("gx", "gy"), None),
        P(("gx", "gy"), None),
        P(("gx", "gy")),
        P(("gx", "gy")),
    )
    out_specs = (P("gy", None, "gx"), P(None, "gy", None, "gx"))
    return jax.shard_map(shards, mesh=mesh, in_specs=in_specs, out_specs=out_specs, check_vma=False)
```
